512 devices in a mesh: vertex: 64 (over z, y), view: 8 (over x, core).
Axes of the slice: x: 4, y: 8, z: 8, core: 2. Of those that a mesh axis runs over, the one named last changes fastest.
Arguments:
- coeffs: bfloat16 [512], P('view'), may hold values from -4 to 4
- shape_basis: bfloat16 [512, 3, 65536], P('view', None, 'vertex'), may hold values from -0.25 to 0.25
- rest_pose: float32 [3, 65536], P(None, 'vertex'), may hold values from -5 to 5
- triangles: int32 [3, 131072], P(None, 'vertex'), may hold values from 0 to 1023
- fetch_list: int32 [512, 64, 4], P(('vertex', 'view')), may hold values from -1 to 15, as said below
- tile_cover: int32 [16384, 8], P(('vertex', 'view')), may hold values from 0 to 255, as said below
- pix_slot: int32 [16384, 256], P(('vertex', 'view')), may hold values from 0 to 1023
- barycentric: float32 [16384, 3, 256], P(('vertex', 'view')), as said below
- camera: float32 [16384, 12], P(('vertex', 'view')), may hold values from -2 to 2
- target: float32 [16384, 3, 256], P(('vertex', 'view')), may hold values from -1 to 1
Outputs:
- photo_loss: float32 [], replicated
- vertex_grad: float32 [3, 65536], P(None, 'vertex')
- coeff_grad: float32 [512], P('view')
The draws below stay inside these ranges and needn't reach their ends.
Inputs may be any that keep to these rules, and one draw needn't show every extreme that they name: Triangle t lies in vertex shard t // 2048; its corners are the vertices triangles[c, t] + (t // 2048) * 1024 of that shard. Let u = o // 8 for owner o. Each row fetch_list[o, h] names distinct blocks of shard h, filled from the front and -1 after. A row is empty unless (h - u) mod 64 is one of j - 3 for j = 0 .. 8 - 2 (taken mod 64) or 32; other rows may be empty too, and every owner has some shard with all 4 entries filled. `tile_cover`: entry e of a tile names entry e % 4 of row e // 4 of the fetch list of the tile's owner (tile t belongs to owner t // 32); that entry is always filled. `pix_slot`: slot q names triangle q % 128 of the block given by the tile's coverage entry q // 128. `barycentric`: the three weights of a pixel are positive and sum to one.
All inputs are finite; a program needn't handle non-finite values.
Results may differ from the reference program's by a relative error of at most 0.0003.
Values sent between devices are 32-bit elements; how exact they have to be, the bound alone decides.
No kernel may reach another device: no remote copies, remote signals or barrier semaphores. Data moves between devices by JAX's collectives and lax.ppermute only.
A program may use at most 64 MiB of HBM per device.

```python
import jax
import jax.numpy as jnp
from jax import lax

K = 512
V_DEV = 1024
BLOCK = 128
CAP = 4
WIN = 8
NB = 8
PIX = 256
TILE_DEV = 32
TB_DEV = 16
HOLDERS = 64
OWNERS = 512
VERTS = 65536
TRIS = 131072
TILES = 16384
PIXELS = 4194304
N_VIEW = 8


def reach_table():
    window_ids = jnp.arange(WIN, dtype=jnp.int32)
    back = (WIN - 2) // 2
    return jnp.where(window_ids == WIN - 1, HOLDERS // 2, window_ids - back).astype(jnp.int32)


def request_counts(key):
    back = (WIN - 2) // 2
    window_counts = jax.random.randint(jax.random.fold_in(key, 101), (OWNERS, WIN), 0, CAP + 1)
    window_ids = jnp.arange(WIN, dtype=jnp.int32)[None, :]
    forced = (window_ids == WIN - 1) | (window_ids == back - 1)
    window_counts = jnp.where(forced, jnp.maximum(window_counts, 1), window_counts)
    full_at = jax.random.randint(jax.random.fold_in(key, 102), (OWNERS, 1), 0, WIN).astype(jnp.int32)
    window_counts = jnp.where(window_ids == full_at, CAP, window_counts).astype(jnp.int32)
    owner_vertex = (jnp.arange(OWNERS, dtype=jnp.int32) // (OWNERS // HOLDERS))[:, None]
    holder_ids = jnp.arange(HOLDERS, dtype=jnp.int32)[None, :]
    relative = (holder_ids - owner_vertex) % HOLDERS
    is_half = relative == HOLDERS // 2
    near_index = (relative + back) % HOLDERS
    window_index = jnp.where(is_half, WIN - 1, near_index)
    inside = is_half | (near_index < WIN - 1)
    picked = jnp.take_along_axis(window_counts, jnp.clip(window_index, 0, WIN - 1), axis=1)
    counts = jnp.where(inside, picked, 0).astype(jnp.int32)
    full_holder = ((owner_vertex + reach_table()[full_at]) % HOLDERS).astype(jnp.int32)
    return (counts, full_holder)


def draw_fetch_list(key, part):
    counts, full_holder = request_counts(key)
    scores = jax.random.randint(jax.random.fold_in(key, 103), (OWNERS, HOLDERS, TB_DEV), 0, 2 ** 16)
    scores = scores * TB_DEV + jnp.arange(TB_DEV, dtype=jnp.int32)
    ranked = jnp.argsort(scores, axis=-1)[:, :, :CAP].astype(jnp.int32)
    slot_ids = jnp.arange(CAP, dtype=jnp.int32)[None, None, :]
    return jnp.where(slot_ids < counts[:, :, None], ranked, -1).astype(jnp.int32)


def draw_tile_cover(key, part):
    back = (WIN - 2) // 2
    counts, full_holder = request_counts(key)
    tile_ids = jnp.arange(TILES, dtype=jnp.int32)
    owner_ids = tile_ids // TILE_DEV
    owner_vertex = owner_ids // (OWNERS // HOLDERS)
    pick_win = jax.random.randint(jax.random.fold_in(key, 104), (TILES, NB), 0, WIN).astype(jnp.int32)
    column_ids = jnp.arange(NB, dtype=jnp.int32)[None, :]
    first_tile = (tile_ids % TILE_DEV == 0)[:, None]
    pick_win = jnp.where(first_tile & (column_ids == 0), WIN - 1, pick_win)
    pick_win = jnp.where(first_tile & (column_ids == 1), back - 1, pick_win)
    pick_holder = (owner_vertex[:, None] + reach_table()[pick_win]) % HOLDERS
    available = counts[owner_ids[:, None], pick_holder]
    fallback = full_holder[owner_ids, 0][:, None]
    pick_holder = jnp.where(available > 0, pick_holder, fallback)
    available = jnp.where(available > 0, available, CAP)
    drawn = jax.random.randint(jax.random.fold_in(key, 105), (TILES, NB), 0, 2 ** 20)
    pick_slot = drawn % available
    return (pick_holder * CAP + pick_slot).astype(jnp.int32)


def draw_barycentric(key, part):
    uniform_raw = jax.random.uniform(key, (TILES, 3, PIX), jnp.float32, 0.05, 1.0)
    weights_raw = uniform_raw * uniform_raw + 0.02
    return weights_raw / jnp.sum(weights_raw, axis=1, keepdims=True)


def plant(array, own_key, smallest, high):
    index_at = [jax.random.randint(jax.random.fold_in(own_key, axis), (), 0, length) for axis, length in enumerate(array.shape)]
    widest = array.shape.index(max(array.shape))
    neighbour = index_at[:widest] + [(index_at[widest] + 1) % array.shape[widest]] + index_at[widest + 1:]
    return array.at[tuple(index_at)].set(smallest).at[tuple(neighbour)].set(high)


def block_scale(rng, dims, cuts, smallest, high):
    loudness = 1.0
    for dim, blocks in cuts:
        draws = jax.random.uniform(jax.random.fold_in(jax.random.fold_in(rng, 6), dim), (blocks,), jnp.float32, smallest / len(cuts), high / len(cuts))
        loudness = loudness * jnp.repeat(jnp.exp(draws), dims[dim] // blocks).reshape((-1,) + (1,) * (len(dims) - 1 - dim))
    return loudness


def centred(own_key, extent, scale, reach, cuts=(), kind=jnp.bfloat16):
    result = jax.random.normal(own_key, extent, jnp.float32) * scale
    if len(cuts) > 0:
        result = block_scale(own_key, extent, cuts, -0.22, 0.18) * result
    return jnp.clip(result, min=-reach, max=reach).astype(kind)


def setup_inputs(seed: int = 0) -> dict:
    splits = jax.random.split(jax.random.key(seed), 11)
    return {
        "coeffs": centred(splits[0], (K,), 1.0, 4.0, ((0, 8),)),
        "shape_basis": centred(splits[1], (K, 3, VERTS), K ** -0.5, 0.25, ((0, 8), (2, 64))),
        "rest_pose": centred(splits[2], (3, VERTS), 1.0, 5.0, ((1, 64),), jnp.float32),
        "triangles": plant(jax.random.randint(splits[3], (3, TRIS), 0, V_DEV), jax.random.fold_in(splits[3], 1), 0, V_DEV - 1).astype(jnp.int32),
        "fetch_list": draw_fetch_list(jax.random.fold_in(splits[10], 71), 0),
        "tile_cover": draw_tile_cover(jax.random.fold_in(splits[10], 71), 0),
        "pix_slot": plant(jax.random.randint(splits[6], (TILES, PIX), 0, NB * BLOCK), jax.random.fold_in(splits[6], 1), 0, (NB * BLOCK) - 1).astype(jnp.int32),
        "barycentric": draw_barycentric(jax.random.fold_in(splits[10], 71), 0),
        "camera": centred(splits[8], (TILES, 12), 0.4, 2.0, ((0, 512),), jnp.float32),
        "target": jnp.clip(jax.random.uniform(splits[9], (TILES, 3, PIX), jnp.float32, -1.0, 1.0) * block_scale(splits[9], (TILES, 3, PIX), ((0, 512),), -0.4, 0.0), -1.0, 1.0),
    }


SMOOTH = 0.1

def photometric(positions, triangles, fetch_list, tile_cover, pix_slot, barycentric, camera, target):
    tile_count = tile_cover.shape[0]
    owner_ids = (jnp.arange(tile_count, dtype=jnp.int32) // TILE_DEV)[:, None]
    entries = jnp.take_along_axis(tile_cover, pix_slot // BLOCK, axis=1)
    holder = entries // CAP
    local_block = fetch_list[owner_ids, holder, entries % CAP]
    triangle_ids = (holder * TB_DEV + local_block) * BLOCK + pix_slot % BLOCK
    surface = barycentric[None, :, 0, :] * positions[:, triangles[0, triangle_ids] + holder * V_DEV]
    surface = surface + barycentric[None, :, 1, :] * positions[:, triangles[1, triangle_ids] + holder * V_DEV]
    surface = surface + barycentric[None, :, 2, :] * positions[:, triangles[2, triangle_ids] + holder * V_DEV]
    matrix = camera[:, :9].reshape(tile_count, 3, 3)
    shifted = camera[:, 9:12]
    linear = matrix[:, :, 0, None] * surface[0][:, None, :]
    linear = linear + matrix[:, :, 1, None] * surface[1][:, None, :]
    linear = linear + matrix[:, :, 2, None] * surface[2][:, None, :]
    linear = linear + shifted[:, :, None]
    shaded = jnp.tanh(linear)
    differ = shaded - target
    return jnp.sum(jnp.sqrt(differ * differ + SMOOTH * SMOOTH))

def reference(coeffs, shape_basis, rest_pose, triangles, fetch_list, tile_cover, pix_slot, barycentric, camera, target):
    flat_basis = shape_basis.reshape(K, 3 * VERTS)
    offset = jnp.dot(coeffs[None, :], flat_basis, preferred_element_type=jnp.float32).reshape(3, VERTS)
    positions = rest_pose + offset
    energy, vertex_grad = jax.value_and_grad(photometric)(positions, triangles, fetch_list, tile_cover, pix_slot, barycentric, camera, target)
    groups = flat_basis.reshape(N_VIEW, K // N_VIEW, 3 * VERTS)
    flat_grad = vertex_grad.reshape(3 * VERTS)

    def project(basis_rows):
        return jnp.dot(basis_rows.astype(jnp.float32), flat_grad, precision=lax.Precision.HIGHEST)
    coeff_grad = lax.map(project, groups).reshape(K)
    return (energy / PIXELS, vertex_grad, coeff_grad)
```

```python
import jax
import jax.numpy as jnp
from jax import lax
from jax.experimental import pallas as pl
from jax.experimental.pallas import tpu as pltpu
from jax.sharding import PartitionSpec as P

LANES = 128
SMOOTH = 0.1
HOLDERS = 64
VIEWS = 8
OFFSETS = (-3, -2, -1, 0, 1, 2, 3, 32)
WIN = len(OFFSETS)
CAP = 4
COVER = 8
TILES = 32
ROW = 9 * LANES

F32 = jnp.float32
BF16 = jnp.bfloat16
VMEM = pl.BlockSpec(memory_space=pltpu.VMEM)
SMEM = pl.BlockSpec(memory_space=pltpu.SMEM)


def holder_of(u, slot):
    return (u + OFFSETS[slot]) & (HOLDERS - 1)


def owner_of(h, slot):
    return (h - OFFSETS[slot]) & (HOLDERS - 1)


def partial_kernel(coeff_ref, basis_ref, out_ref):
    total = jnp.zeros(basis_ref.shape[1:], F32)
    for k in range(basis_ref.shape[0]):
        total = total + coeff_ref[k] * basis_ref[k].astype(F32)
    for v in range(VIEWS):
        out_ref[v] = total[:, v * LANES : (v + 1) * LANES]


def holder_kernel(parts_ref, rest_ref, corner_ref, out_ref):
    position = rest_ref[...]
    for v in range(VIEWS):
        position = position + parts_ref[v]
    for row in range(9):
        value = position[row : row + 1] if row < 3 else corner_ref[row - 3 : row - 2]
        out_ref[:, :, row * LANES : (row + 1) * LANES] = jnp.broadcast_to(
            value[None], (HOLDERS, 1, LANES)
        )


def window_kernel(u_ref, slices_ref, out_ref):
    u = u_ref[0]
    for slot in range(WIN):
        value = slices_ref[pl.ds(holder_of(u, slot), 1)]
        out_ref[:, :, slot * ROW : (slot + 1) * ROW] = jnp.broadcast_to(value, (VIEWS, 1, ROW))


def pick_lanes(source, lane):
    return jnp.take_along_axis(source, lane, axis=1, mode="promise_in_bounds")


def high_low(values):
    high = values.astype(BF16).astype(F32)
    return jnp.concatenate([high, values - high], axis=0).astype(BF16)


def lane_onehot(lane_row):
    ids = lax.broadcasted_iota(jnp.int32, (LANES, LANES), 0)
    return jnp.where(ids == lane_row, 1.0, 0.0).astype(BF16)


def dot_nt(a, b):
    return lax.dot_general(a, b, (((1,), (1,)), ((), ())), preferred_element_type=F32)


def tile_kernel(
    block_ref,
    entry_ref,
    entry_row_ref,
    table_ref,
    slot_ref,
    weight_ref,
    camera_ref,
    target_ref,
    out_ref,
    energy_ref,
    slot_rows,
    corner_id,
    entry_table,
    corner_pix,
    grad_pix,
    tile_grad,
    entry_grad,
):
    sub8 = lax.broadcasted_iota(jnp.int32, (8, LANES), 0)
    for half in range(2):
        slot_rows[half * TILES : (half + 1) * TILES, :] = slot_ref[
            :, half * LANES : (half + 1) * LANES
        ]
    for j in range(WIN):
        for s in range(CAP):
            block = block_ref[j, s]
            for c in range(3):
                at = pl.multiple_of(
                    j * ROW + 3 * LANES + (2 * c + (block & 1)) * LANES, LANES
                )
                ids = table_ref[pl.ds(block >> 1, 1), 0, pl.ds(at, LANES)]
                corner_id[pl.ds(j * 16 + c * CAP + s, 1), :] = ids.astype(jnp.int32)
    for j in range(WIN):
        ids = [corner_id[pl.ds(j * 16 + 8 * i, 8), :] for i in range(2)]
        lane = [i & (LANES - 1) for i in ids]
        sub = [i >> 7 for i in ids]
        for d in range(3):
            at = j * ROW + d * LANES
            found = [jnp.zeros((8, LANES), F32)] * 2
            for s in range(8):
                source = jnp.broadcast_to(table_ref[s, :, at : at + LANES], (8, LANES))
                for i in range(2):
                    found[i] = jnp.where(sub[i] == s, pick_lanes(source, lane[i]), found[i])
            for c in range(3):
                rows = found[c // 2][(c % 2) * CAP : (c % 2) * CAP + CAP]
                entry_table[pl.ds(j * 64 + 3 * c + d, CAP, stride=16), :] = rows

    def gather_tile(t, carry):
        for half in range(2):
            q = slot_rows[pl.ds(half * TILES + t, 1), :]
            q = jnp.broadcast_to(q, (8, LANES))
            lane = q & (LANES - 1)
            which = q >> 7
            first = jnp.zeros((8, LANES), F32)
            second = jnp.zeros((8, LANES), F32)
            for n in range(COVER):
                at = pl.multiple_of(entry_ref[t, n] * 16, 16)
                mine = which == n
                first = jnp.where(mine, pick_lanes(entry_table[pl.ds(at, 8), :], lane), first)
                second = jnp.where(
                    mine, pick_lanes(entry_table[pl.ds(at + 8, 8), :], lane), second
                )
            row = half * TILES + t
            corner_pix[pl.ds(row, 8, stride=2 * TILES), :] = first
            corner_pix[pl.ds(8 * 2 * TILES + row, 1), :] = second[0:1]
        return carry

    lax.fori_loop(0, TILES, gather_tile, 0, unroll=2)

    energy = jnp.zeros((TILES, LANES), F32)
    for half in range(2):
        cols = slice(half * LANES, (half + 1) * LANES)
        weights = [weight_ref[:, c, cols] for c in range(3)]

        def rows_of(cd):
            return pl.ds(cd * 2 * TILES + half * TILES, TILES)

        surface = []
        for d in range(3):
            value = weights[0] * corner_pix[rows_of(d), :]
            value = value + weights[1] * corner_pix[rows_of(3 + d), :]
            surface.append(value + weights[2] * corner_pix[rows_of(6 + d), :])
        grad_surface = [jnp.zeros((TILES, LANES), F32)] * 3
        for r in range(3):
            linear = camera_ref[:, 3 * r : 3 * r + 1] * surface[0]
            linear = linear + camera_ref[:, 3 * r + 1 : 3 * r + 2] * surface[1]
            linear = linear + camera_ref[:, 3 * r + 2 : 3 * r + 3] * surface[2]
            shaded = jnp.tanh(linear + camera_ref[:, 9 + r : 10 + r])
            differ = shaded - target_ref[:, r, cols]
            spread = jnp.sqrt(differ * differ + SMOOTH * SMOOTH)
            energy = energy + spread
            grad_linear = differ / spread * (1.0 - shaded * shaded)
            for d in range(3):
                grad_surface[d] = (
                    grad_surface[d] + camera_ref[:, 3 * r + d : 3 * r + d + 1] * grad_linear
                )
        for c in range(3):
            for d in range(3):
                grad_pix[rows_of(3 * c + d), :] = weights[c] * grad_surface[d]
    energy_ref[...] = jnp.sum(energy, axis=0, keepdims=True)

    def scatter_tile(t, carry):
        spread_rows = [[] for _ in range(9)]
        onehot = []
        for half in range(2):
            q = slot_rows[pl.ds(half * TILES + t, 1), :]
            mine = jnp.broadcast_to(q >> 7, (8, LANES)) == sub8
            onehot.append(lane_onehot(jnp.broadcast_to(q & (LANES - 1), (LANES, LANES))))
            for cd in range(9):
                grad = grad_pix[pl.ds(cd * 2 * TILES + half * TILES + t, 1), :]
                grad = jnp.broadcast_to(grad, (8, LANES))
                spread_rows[cd].append(jnp.where(mine, grad, 0.0))
        rows = jnp.concatenate([jnp.concatenate(r, axis=1) for r in spread_rows], axis=0)
        summed = dot_nt(high_low(rows), jnp.concatenate(onehot, axis=1))
        summed = summed[:72] + summed[72:]
        at = pl.multiple_of(t * 8, 8)
        for cd in range(9):
            tile_grad[pl.ds(at, 8), cd * LANES : (cd + 1) * LANES] = summed[8 * cd : 8 * cd + 8]
        return carry

    lax.fori_loop(0, TILES, scatter_tile, 0, unroll=2)

    entry_ids = lax.broadcasted_iota(jnp.int32, (WIN * CAP, TILES * COVER), 0)
    pick = jnp.where(entry_ids == entry_row_ref[...], 1.0, 0.0).astype(BF16)
    values = tile_grad[...]
    high = values.astype(BF16)
    low = (values - high.astype(F32)).astype(BF16)
    entry_grad[...] = jnp.dot(pick, high, preferred_element_type=F32) + jnp.dot(
        pick, low, preferred_element_type=F32
    )

    for j in range(WIN):
        rows = [[] for _ in range(3)]
        onehot = []
        for c in range(3):
            for s in range(CAP):
                ids = corner_id[pl.ds(j * 16 + c * CAP + s, 1), :]
                mine = jnp.broadcast_to(ids >> 7, (8, LANES)) == sub8
                onehot.append(
                    lane_onehot(jnp.broadcast_to(ids & (LANES - 1), (LANES, LANES)))
                )
                for d in range(3):
                    at = (3 * c + d) * LANES
                    grad = entry_grad[pl.ds(j * CAP + s, 1), at : at + LANES]
                    rows[d].append(jnp.where(mine, jnp.broadcast_to(grad, (8, LANES)), 0.0))
        stacked = jnp.concatenate([jnp.concatenate(r, axis=1) for r in rows], axis=0)
        summed = dot_nt(high_low(stacked), jnp.concatenate(onehot, axis=1))
        for d in range(3):
            out_ref[:, j * 3 + d, :] = summed[8 * d : 8 * d + 8] + summed[24 + 8 * d : 32 + 8 * d]


def owner_sum_kernel(u_ref, parts_ref, out_ref):
    u = u_ref[0]
    total = parts_ref[0]
    for v in range(1, VIEWS):
        total = total + parts_ref[v]
    out_ref[...] = jnp.zeros(out_ref.shape, F32)
    for slot in range(WIN):
        for d in range(3):
            row = slot * 3 + d
            out_ref[pl.ds(holder_of(u, slot), 1), :, d * LANES : (d + 1) * LANES] = total[
                row : row + 1
            ][None]


def holder_sum_kernel(u_ref, parts_ref, energy_ref, out_ref):
    h = u_ref[0]
    total = parts_ref[pl.ds(owner_of(h, 0), 1)]
    for slot in range(1, WIN):
        total = total + parts_ref[pl.ds(owner_of(h, slot), 1)]
    out_ref[:, :, : 3 * LANES] = jnp.broadcast_to(total, (VIEWS, 1, 3 * LANES))
    out_ref[:, :, 3 * LANES :] = jnp.broadcast_to(energy_ref[...][None], (VIEWS, 1, LANES))


def project_kernel(slices_ref, basis_ref, grad_ref, out_ref):
    shapes = basis_ref.shape[0]
    total = jnp.zeros((shapes, 3, LANES), F32)
    energy = jnp.zeros((1, LANES), F32)
    for v in range(VIEWS):
        cols = slice(v * LANES, (v + 1) * LANES)
        for d in range(3):
            grad_ref[d : d + 1, cols] = slices_ref[v, :, d * LANES : (d + 1) * LANES]
        energy = energy + slices_ref[v, :, 3 * LANES :]
        total = total + basis_ref[:, :, cols].astype(F32) * grad_ref[:, cols][None]
    lanes = jnp.sum(total, axis=1)
    row = lax.dot_general(
        jnp.ones((8, LANES), F32),
        lanes,
        (((1,), (1,)), ((), ())),
        precision=lax.Precision.HIGHEST,
        preferred_element_type=F32,
    )[0:1]
    row = jnp.concatenate([row, jnp.zeros((1, LANES - shapes), F32)], axis=1)
    out_ref[:, :, :LANES] = jnp.broadcast_to(row[None], (HOLDERS, 1, LANES))
    out_ref[:, :, LANES:] = jnp.broadcast_to(energy[None], (HOLDERS, 1, LANES))


def call(kernel, out_shapes, args, scalars=0, scratch=(), name=None):
    shapes = [jax.ShapeDtypeStruct(s, F32) for s in out_shapes]
    single = len(shapes) == 1
    return pl.pallas_call(
        kernel,
        out_shape=shapes[0] if single else shapes,
        in_specs=[SMEM] * scalars + [VMEM] * (len(args) - scalars),
        out_specs=VMEM if single else [VMEM] * len(shapes),
        scratch_shapes=list(scratch),
        name=name,
    )(*args)


def exchange(array, axis):
    return lax.all_to_all(array, axis, 0, 0, tiled=True)


def tile_call(block_ids, entries, table, pix_slot, barycentric, camera, target):
    return call(
        tile_kernel,
        [(VIEWS, 3 * WIN, LANES), (1, LANES)],
        (
            block_ids,
            entries,
            entries.reshape(1, TILES * COVER),
            table,
            pix_slot,
            barycentric,
            camera,
            target,
        ),
        scalars=2,
        scratch=(
            pltpu.VMEM((2 * TILES, LANES), jnp.int32),
            pltpu.VMEM((16 * WIN, LANES), jnp.int32),
            pltpu.VMEM((16 * WIN * CAP, LANES), F32),
            pltpu.VMEM((9 * 2 * TILES, LANES), F32),
            pltpu.VMEM((9 * 2 * TILES, LANES), F32),
            pltpu.VMEM((TILES * COVER, 9 * LANES), F32),
            pltpu.VMEM((WIN * CAP, 9 * LANES), F32),
        ),
        name="tiles",
    )


def own_requests(u, fetch_list, tile_cover):
    doubled = jnp.concatenate([fetch_list[0], fetch_list[0]], axis=0)
    near = lax.dynamic_slice(doubled, ((u - 3) & (HOLDERS - 1), 0), (WIN - 1, CAP))
    far = lax.dynamic_slice(doubled, ((u + 32) & (HOLDERS - 1), 0), (1, CAP))
    block_ids = jnp.maximum(jnp.concatenate([near, far], axis=0), 0)
    relative = ((tile_cover >> 2) - u + 3) & (HOLDERS - 1)
    entries = jnp.minimum(relative, WIN - 1) * CAP + (tile_cover & (CAP - 1))
    return block_ids, entries


def per_device(
    coeffs,
    shape_basis,
    rest_pose,
    triangles,
    fetch_list,
    tile_cover,
    pix_slot,
    barycentric,
    camera,
    target,
):
    u = lax.axis_index("vertex").astype(jnp.int32)
    view = lax.axis_index("view").astype(jnp.int32)
    u_array = u.reshape(1)
    pixels = (
        tile_cover.shape[0] * pix_slot.shape[1] * lax.axis_size("vertex") * lax.axis_size("view")
    )

    partial = call(
        partial_kernel,
        [(VIEWS, 3, LANES)],
        (coeffs.astype(F32), shape_basis),
        scalars=1,
        name="offsets",
    )
    parts = exchange(partial, "view")
    rest = lax.dynamic_slice(rest_pose, (0, view * LANES), (3, LANES))
    corners = lax.dynamic_slice(triangles, (0, view * 2 * LANES), (3, 2 * LANES))
    corners = corners.reshape(6, LANES).astype(F32)
    slices = call(
        holder_kernel, [(HOLDERS, 1, ROW)], (parts, rest, corners), name="holder"
    )
    slices = exchange(slices, "vertex")
    table = call(
        window_kernel, [(VIEWS, 1, WIN * ROW)], (u_array, slices), scalars=1, name="window"
    )
    table = exchange(table, "view")

    block_ids, entries = own_requests(u, fetch_list, tile_cover)
    parts, energy = tile_call(
        block_ids, entries, table, pix_slot, barycentric, camera, target
    )

    parts = exchange(parts, "view")
    parts = call(
        owner_sum_kernel, [(HOLDERS, 1, 3 * LANES)], (u_array, parts), scalars=1, name="owner_sum"
    )
    parts = exchange(parts, "vertex")
    slices = call(
        holder_sum_kernel,
        [(VIEWS, 1, 4 * LANES)],
        (u_array, parts, energy),
        scalars=1,
        name="holder_sum",
    )
    slices = exchange(slices, "view")
    vertex_grad, rows = call(
        project_kernel,
        [(3, VIEWS * LANES), (HOLDERS, 1, 2 * LANES)],
        (slices, shape_basis),
        name="project",
    )
    total = exchange(rows, "vertex").sum(axis=(0, 1))
    coeff_grad = total[: coeffs.shape[0]]
    energy = jnp.sum(total[LANES:])
    return (energy / pixels, vertex_grad, coeff_grad)


def solution(mesh):
    placed = (
        P("view"),
        P("view", None, "vertex"),
        P(None, "vertex"),
        P(None, "vertex"),
        P(("vertex", "view"), None, None),
        P(("vertex", "view"), None),
        P(("vertex", "view"), None),
        P(("vertex", "view"), None, None),
        P(("vertex", "view"), None),
        P(("vertex", "view"), None, None),
    )
    return jax.shard_map(
        per_device,
        mesh=mesh,
        in_specs=placed,
        out_specs=(P(), P(None, "vertex"), P("view")),
        check_vma=False,
    )
```

```python
import jax
import jax.numpy as jnp
from jax import lax
from jax.experimental import pallas as pl
from jax.experimental.pallas import tpu as pltpu
from jax.sharding import PartitionSpec as P

LANES = 128
SMOOTH = 0.1
VIEWS = 8
OFFSETS = (-3, -2, -1, 0, 1, 2, 3, 32)
WIN = len(OFFSETS)
CAP = 4
COVER = 8
TILES = 32
BLOCKS = 16
SHARD = 24 + 3 * BLOCKS

F32 = jnp.float32
BF16 = jnp.bfloat16
VMEM = pl.BlockSpec(memory_space=pltpu.VMEM)
SMEM = pl.BlockSpec(memory_space=pltpu.SMEM)


def pick_lanes(source, lane):
    return jnp.take_along_axis(source, lane, axis=1, mode="promise_in_bounds")


def high_low(values):
    high = values.astype(BF16).astype(F32)
    return jnp.concatenate([high, values - high], axis=0).astype(BF16)


def lane_onehot(lane_row):
    ids = lax.broadcasted_iota(jnp.int32, (LANES, LANES), 0)
    return jnp.where(ids == lane_row, 1.0, 0.0).astype(BF16)


def dot_nt(a, b):
    return lax.dot_general(a, b, (((1,), (1,)), ((), ())), preferred_element_type=F32)


def tile_kernel(
    block_ref,
    entry_ref,
    entry_row_ref,
    table_ref,
    slot_ref,
    weight_ref,
    camera_ref,
    target_ref,
    out_ref,
    energy_ref,
    slot_rows,
    corner_id,
    entry_table,
    corner_pix,
    grad_pix,
    tile_grad,
    entry_grad,
):
    sub8 = lax.broadcasted_iota(jnp.int32, (8, LANES), 0)
    for half in range(2):
        slot_rows[half * TILES : (half + 1) * TILES, :] = slot_ref[
            :, half * LANES : (half + 1) * LANES
        ]
    for j in range(WIN):
        for s in range(CAP):
            block = block_ref[j, s]
            for c in range(3):
                ids = table_ref[j, pl.ds(24 + c * BLOCKS + block, 1), :]
                corner_id[pl.ds(j * 16 + c * CAP + s, 1), :] = ids.astype(jnp.int32)
    for j in range(WIN):
        ids = [corner_id[pl.ds(j * 16 + 8 * i, 8), :] for i in range(2)]
        lane = [i & (LANES - 1) for i in ids]
        sub = [i >> 7 for i in ids]
        for d in range(3):
            found = [jnp.zeros((8, LANES), F32)] * 2
            for s in range(8):
                source = jnp.broadcast_to(table_ref[j, 8 * d + s : 8 * d + s + 1, :], (8, LANES))
                for i in range(2):
                    found[i] = jnp.where(sub[i] == s, pick_lanes(source, lane[i]), found[i])
            for c in range(3):
                rows = found[c // 2][(c % 2) * CAP : (c % 2) * CAP + CAP]
                entry_table[pl.ds(j * 64 + 3 * c + d, CAP, stride=16), :] = rows

    def gather_tile(t, carry):
        for half in range(2):
            q = slot_rows[pl.ds(half * TILES + t, 1), :]
            q = jnp.broadcast_to(q, (8, LANES))
            lane = q & (LANES - 1)
            which = q >> 7
            first = jnp.zeros((8, LANES), F32)
            second = jnp.zeros((8, LANES), F32)
            for n in range(COVER):
                at = pl.multiple_of(entry_ref[t, n] * 16, 16)
                mine = which == n
                first = jnp.where(mine, pick_lanes(entry_table[pl.ds(at, 8), :], lane), first)
                second = jnp.where(
                    mine, pick_lanes(entry_table[pl.ds(at + 8, 8), :], lane), second
                )
            row = half * TILES + t
            corner_pix[pl.ds(row, 8, stride=2 * TILES), :] = first
            corner_pix[pl.ds(8 * 2 * TILES + row, 1), :] = second[0:1]
        return carry

    lax.fori_loop(0, TILES, gather_tile, 0, unroll=2)

    energy = jnp.zeros((TILES, LANES), F32)
    for half in range(2):
        cols = slice(half * LANES, (half + 1) * LANES)
        weights = [weight_ref[c, :, cols] for c in range(3)]

        def rows_of(cd):
            return pl.ds(cd * 2 * TILES + half * TILES, TILES)

        surface = []
        for d in range(3):
            value = weights[0] * corner_pix[rows_of(d), :]
            value = value + weights[1] * corner_pix[rows_of(3 + d), :]
            surface.append(value + weights[2] * corner_pix[rows_of(6 + d), :])
        grad_surface = [jnp.zeros((TILES, LANES), F32)] * 3
        for r in range(3):
            linear = camera_ref[:, 3 * r : 3 * r + 1] * surface[0]
            linear = linear + camera_ref[:, 3 * r + 1 : 3 * r + 2] * surface[1]
            linear = linear + camera_ref[:, 3 * r + 2 : 3 * r + 3] * surface[2]
            shaded = jnp.tanh(linear + camera_ref[:, 9 + r : 10 + r])
            differ = shaded - target_ref[r, :, cols]
            spread = jnp.sqrt(differ * differ + SMOOTH * SMOOTH)
            energy = energy + spread
            grad_linear = differ / spread * (1.0 - shaded * shaded)
            for d in range(3):
                grad_surface[d] = (
                    grad_surface[d] + camera_ref[:, 3 * r + d : 3 * r + d + 1] * grad_linear
                )
        for c in range(3):
            for d in range(3):
                grad_pix[rows_of(3 * c + d), :] = weights[c] * grad_surface[d]
    energy_ref[...] = energy[0:8] + energy[8:16] + energy[16:24] + energy[24:32]

    def scatter_tile(t, carry):
        spread_rows = [[] for _ in range(9)]
        onehot = []
        for half in range(2):
            q = slot_rows[pl.ds(half * TILES + t, 1), :]
            mine = jnp.broadcast_to(q >> 7, (8, LANES)) == sub8
            onehot.append(lane_onehot(jnp.broadcast_to(q & (LANES - 1), (LANES, LANES))))
            for cd in range(9):
                grad = grad_pix[pl.ds(cd * 2 * TILES + half * TILES + t, 1), :]
                grad = jnp.broadcast_to(grad, (8, LANES))
                spread_rows[cd].append(jnp.where(mine, grad, 0.0))
        rows = jnp.concatenate([jnp.concatenate(r, axis=1) for r in spread_rows], axis=0)
        summed = dot_nt(high_low(rows), jnp.concatenate(onehot, axis=1))
        summed = summed[:72] + summed[72:]
        at = pl.multiple_of(t * 8, 8)
        for cd in range(9):
            tile_grad[pl.ds(at, 8), cd * LANES : (cd + 1) * LANES] = summed[8 * cd : 8 * cd + 8]
        return carry

    lax.fori_loop(0, TILES, scatter_tile, 0, unroll=2)

    entry_ids = lax.broadcasted_iota(jnp.int32, (WIN * CAP, TILES * COVER), 0)
    pick = jnp.where(entry_ids == entry_row_ref[...], 1.0, 0.0).astype(BF16)
    values = tile_grad[...]
    high = values.astype(BF16)
    low = (values - high.astype(F32)).astype(BF16)
    entry_grad[...] = jnp.dot(pick, high, preferred_element_type=F32) + jnp.dot(
        pick, low, preferred_element_type=F32
    )

    for j in range(WIN):
        rows = [[] for _ in range(3)]
        onehot = []
        for c in range(3):
            for s in range(CAP):
                ids = corner_id[pl.ds(j * 16 + c * CAP + s, 1), :]
                mine = jnp.broadcast_to(ids >> 7, (8, LANES)) == sub8
                onehot.append(
                    lane_onehot(jnp.broadcast_to(ids & (LANES - 1), (LANES, LANES)))
                )
                for d in range(3):
                    at = (3 * c + d) * LANES
                    grad = entry_grad[pl.ds(j * CAP + s, 1), at : at + LANES]
                    rows[d].append(jnp.where(mine, jnp.broadcast_to(grad, (8, LANES)), 0.0))
        stacked = jnp.concatenate([jnp.concatenate(r, axis=1) for r in rows], axis=0)
        summed = dot_nt(high_low(stacked), jnp.concatenate(onehot, axis=1))
        for d in range(3):
            out_ref[j, 8 * d : 8 * d + 8, :] = (
                summed[8 * d : 8 * d + 8] + summed[24 + 8 * d : 32 + 8 * d]
            )


def call(kernel, out_shapes, args, scalars=0, scratch=(), name=None):
    shapes = [jax.ShapeDtypeStruct(s, F32) for s in out_shapes]
    single = len(shapes) == 1
    return pl.pallas_call(
        kernel,
        out_shape=shapes[0] if single else shapes,
        in_specs=[SMEM] * scalars + [VMEM] * (len(args) - scalars),
        out_specs=VMEM if single else [VMEM] * len(shapes),
        scratch_shapes=list(scratch),
        name=name,
    )(*args)


def exchange(array, axis):
    return lax.all_to_all(array, axis, 0, 0, tiled=True)


def tile_call(block_ids, entries, table, pix_slot, barycentric, camera, target):
    return call(
        tile_kernel,
        [(WIN, 24, LANES), (8, LANES)],
        (
            block_ids,
            entries,
            entries.reshape(1, TILES * COVER),
            table,
            pix_slot,
            barycentric,
            camera,
            target,
        ),
        scalars=2,
        scratch=(
            pltpu.VMEM((2 * TILES, LANES), jnp.int32),
            pltpu.VMEM((16 * WIN, LANES), jnp.int32),
            pltpu.VMEM((16 * WIN * CAP, LANES), F32),
            pltpu.VMEM((9 * 2 * TILES, LANES), F32),
            pltpu.VMEM((9 * 2 * TILES, LANES), F32),
            pltpu.VMEM((TILES * COVER, 9 * LANES), F32),
            pltpu.VMEM((WIN * CAP, 9 * LANES), F32),
        ),
        name="tiles",
    )


def own_requests(u, fetch_list, tile_cover):
    holders = fetch_list.shape[1]
    doubled = jnp.concatenate([fetch_list[0], fetch_list[0]], axis=0)
    near = lax.dynamic_slice(doubled, ((u - 3) & (holders - 1), 0), (WIN - 1, CAP))
    far = lax.dynamic_slice(doubled, ((u + 32) & (holders - 1), 0), (1, CAP))
    block_ids = jnp.maximum(jnp.concatenate([near, far], axis=0), 0)
    relative = ((tile_cover >> 2) - u + 3) & (holders - 1)
    entries = jnp.minimum(relative, WIN - 1) * CAP + (tile_cover & (CAP - 1))
    return block_ids, entries


def to_all(array, axis):
    size = lax.axis_size(axis)
    return exchange(jnp.broadcast_to(array[None], (size, *array.shape)), axis)


def along_window(array, sign):
    holders = lax.axis_size("vertex")
    pairs = [
        (h * VIEWS + j, (h + sign * OFFSETS[j]) % holders * VIEWS + j)
        for h in range(holders)
        for j in range(VIEWS)
    ]
    return lax.ppermute(array, ("vertex", "view"), pairs)


def per_device(
    coeffs,
    shape_basis,
    rest_pose,
    triangles,
    fetch_list,
    tile_cover,
    pix_slot,
    barycentric,
    camera,
    target,
):
    u = lax.axis_index("vertex").astype(jnp.int32)
    pixels = (
        tile_cover.shape[0] * pix_slot.shape[1] * lax.axis_size("vertex") * lax.axis_size("view")
    )
    shapes = coeffs.shape[0]
    basis = jnp.transpose(shape_basis, (1, 0, 2))
    corners = triangles.reshape(3 * BLOCKS, LANES).astype(F32)
    block_ids, entries = own_requests(u, fetch_list, tile_cover)

    partial = jnp.sum(coeffs.astype(F32)[None, :, None] * basis.astype(F32), axis=1)
    partial = lax.optimization_barrier(partial).reshape(24, LANES)
    positions = rest_pose.reshape(24, LANES) + to_all(partial, "view").sum(axis=0)
    shard = along_window(jnp.concatenate([positions, corners], axis=0), -1)
    table = to_all(shard, "view")
    parts, energy = tile_call(
        block_ids,
        entries,
        table,
        pix_slot,
        jnp.transpose(barycentric, (1, 0, 2)),
        camera,
        jnp.transpose(target, (1, 0, 2)),
    )
    returned = along_window(exchange(parts, "view").sum(axis=0), 1)
    total = to_all(jnp.concatenate([returned, energy], axis=0), "view").sum(axis=0)
    vertex_grad = total[:24].reshape(3, VIEWS * LANES)
    coeff_part = jnp.sum(basis.astype(F32) * vertex_grad[:, None, :], axis=(0, 2))
    energy_part = total[24:].sum(axis=0)
    energy_part = energy_part[:shapes] + energy_part[shapes:]
    rows = jnp.concatenate([coeff_part, energy_part]).reshape(1, 2 * shapes)
    total = to_all(rows, "vertex").sum(axis=(0, 1))
    return (jnp.sum(total[shapes:]) / pixels, vertex_grad, total[:shapes])


def solution(mesh):
    placed = (
        P("view"),
        P("view", None, "vertex"),
        P(None, "vertex"),
        P(None, "vertex"),
        P(("vertex", "view"), None, None),
        P(("vertex", "view"), None),
        P(("vertex", "view"), None),
        P(("vertex", "view"), None, None),
        P(("vertex", "view"), None),
        P(("vertex", "view"), None, None),
    )
    return jax.shard_map(
        per_device,
        mesh=mesh,
        in_specs=placed,
        out_specs=(P(), P(None, "vertex"), P("view")),
        check_vma=False,
    )
```

```python
import jax
import jax.numpy as jnp
from jax import lax
from jax.experimental import pallas as pl
from jax.experimental.pallas import tpu as pltpu
from jax.sharding import PartitionSpec as P

LANES = 128
SMOOTH = 0.1
VIEWS = 8
HOLDERS = 64
UNROLL_GATHER = 32
UNROLL_SCATTER = 32
OFFSETS = (-3, -2, -1, 0, 1, 2, 3, 32)
WIN = len(OFFSETS)
CAP = 4
COVER = 8
TILES = 32
BLOCKS = 16
SHARD = 24 + 3 * BLOCKS

F32 = jnp.float32
BF16 = jnp.bfloat16
VMEM = pl.BlockSpec(memory_space=pltpu.VMEM)
SMEM = pl.BlockSpec(memory_space=pltpu.SMEM)


def pick_lanes(source, lane):
    return jnp.take_along_axis(source, lane, axis=1, mode="promise_in_bounds")


def high_low(values):
    high = values.astype(BF16).astype(F32)
    return jnp.concatenate([high, values - high], axis=0).astype(BF16)


def lane_onehot(lane_row, ids):
    row = jnp.broadcast_to(lane_row.astype(F32), (16, LANES)).astype(BF16)
    one = jnp.ones((16, LANES), BF16)
    zero = jnp.zeros((16, LANES), BF16)
    return jnp.concatenate([jnp.where(i == row, one, zero) for i in ids], axis=0)


def dot_nt(a, b):
    return lax.dot_general(a, b, (((1,), (1,)), ((), ())), preferred_element_type=F32)


def entry_of(cover, u):
    relative = ((cover >> 2) - u + 3) & (HOLDERS - 1)
    return jnp.minimum(relative, WIN - 1) * CAP + (cover & (CAP - 1))


def tile_kernel(
    u_ref,
    fetch_ref,
    cover_ref,
    cover_rows_ref,
    table_ref,
    slot_ref,
    weight_ref,
    camera_ref,
    target_ref,
    out_ref,
    energy_ref,
    slot_rows,
    corner_id,
    entry_table,
    last_table,
    tile_last,
    corner_pix,
    grad_pix,
    tile_grad,
    entry_grad,
):
    u = u_ref[0]
    sub8 = lax.broadcasted_iota(jnp.int32, (8, LANES), 0)
    sub16 = lax.broadcasted_iota(jnp.int32, (16, LANES), 0)
    ids16 = [(sub16 + 16 * i).astype(F32).astype(BF16) for i in range(8)]
    for half in range(2):
        slot_rows[half * TILES : (half + 1) * TILES, :] = slot_ref[
            :, half * LANES : (half + 1) * LANES
        ]
    for j in range(WIN):
        for s in range(CAP):
            block = jnp.maximum(fetch_ref[s, (u + OFFSETS[j]) & (HOLDERS - 1)], 0)
            for c in range(3):
                ids = table_ref[j, pl.ds(24 + c * BLOCKS + block, 1), :]
                corner_id[pl.ds(j * 16 + c * CAP + s, 1), :] = ids.astype(jnp.int32)
    for j in range(WIN):
        ids = [corner_id[pl.ds(j * 16 + 8 * i, 8), :] for i in range(2)]
        lane = [i & (LANES - 1) for i in ids]
        sub = [i >> 7 for i in ids]
        for d in range(3):
            found = [jnp.zeros((8, LANES), F32)] * 2
            for s in range(8):
                source = jnp.broadcast_to(
                    table_ref[j, 8 * d + s : 8 * d + s + 1, :], (8, LANES)
                )
                for i in range(2):
                    found[i] = jnp.where(sub[i] == s, pick_lanes(source, lane[i]), found[i])
            for c in range(3):
                rows = found[c // 2][(c % 2) * CAP : (c % 2) * CAP + CAP]
                if 3 * c + d < 8:
                    entry_table[pl.ds(j * 32 + 3 * c + d, CAP, stride=8), :] = rows
                else:
                    last_table[pl.ds(j * CAP, CAP), :] = rows

    def gather_tile(t, carry):
        entries = [entry_of(cover_ref[n, t], u) for n in range(COVER)]
        base = pl.multiple_of(t * 8, 8)
        for n in range(COVER):
            tile_last[pl.ds(base + n, 1), :] = last_table[pl.ds(entries[n], 1), :]
        last = tile_last[pl.ds(base, 8), :]
        for half in range(2):
            q = slot_rows[pl.ds(half * TILES + t, 1), :]
            q = jnp.broadcast_to(q, (8, LANES))
            lane = q & (LANES - 1)
            which = q >> 7
            first = jnp.zeros((8, LANES), F32)
            for n in range(COVER):
                at = pl.multiple_of(entries[n] * 8, 8)
                picked = pick_lanes(entry_table[pl.ds(at, 8), :], lane)
                first = jnp.where(which == n, picked, first)
            second = jnp.where(which == sub8, pick_lanes(last, lane), 0.0)
            row = half * TILES + t
            corner_pix[pl.ds(row, 8, stride=2 * TILES), :] = first
            corner_pix[pl.ds(8 * 2 * TILES + row, 1), :] = jnp.sum(
                second, axis=0, keepdims=True
            )
        return carry

    lax.fori_loop(0, TILES, gather_tile, 0, unroll=UNROLL_GATHER)

    camera = camera_ref[...].T
    energy = jnp.zeros((TILES, LANES), F32)
    for half in range(2):
        cols = slice(half * LANES, (half + 1) * LANES)
        weights = [weight_ref[c, :, cols] for c in range(3)]

        def rows_of(cd):
            return pl.ds(cd * 2 * TILES + half * TILES, TILES)

        surface = []
        for d in range(3):
            value = weights[0] * corner_pix[rows_of(d), :]
            value = value + weights[1] * corner_pix[rows_of(3 + d), :]
            surface.append(value + weights[2] * corner_pix[rows_of(6 + d), :])
        grad_surface = [jnp.zeros((TILES, LANES), F32)] * 3
        for r in range(3):
            matrix = [camera[:, 3 * r + d : 3 * r + d + 1] for d in range(3)]
            linear = matrix[0] * surface[0]
            linear = linear + matrix[1] * surface[1]
            linear = linear + matrix[2] * surface[2]
            shaded = jnp.tanh(linear + camera[:, 9 + r : 10 + r])
            differ = shaded - target_ref[r, :, cols]
            square = differ * differ + SMOOTH * SMOOTH
            inverse = lax.rsqrt(square)
            energy = energy + square * inverse
            grad_linear = differ * inverse * (1.0 - shaded * shaded)
            for d in range(3):
                grad_surface[d] = grad_surface[d] + matrix[d] * grad_linear
        for c in range(3):
            for d in range(3):
                grad = weights[c] * grad_surface[d]
                high = grad.astype(BF16).astype(F32)
                grad_pix[rows_of(3 * c + d), :] = high
                grad_pix[rows_of(9 + 3 * c + d), :] = grad - high
    energy_ref[...] = energy[0:8] + energy[8:16] + energy[16:24] + energy[24:32]

    def scatter_tile(t, carry):
        spread_rows = [[] for _ in range(18)]
        onehot = []
        for half in range(2):
            q = slot_rows[pl.ds(half * TILES + t, 1), :]
            mine = jnp.broadcast_to(q >> 7, (8, LANES)) == sub8
            onehot.append(lane_onehot(q & (LANES - 1), ids16))
            for cd in range(18):
                grad = grad_pix[pl.ds(cd * 2 * TILES + half * TILES + t, 1), :]
                grad = jnp.broadcast_to(grad, (8, LANES))
                spread_rows[cd].append(jnp.where(mine, grad, 0.0))
        rows = jnp.concatenate([jnp.concatenate(r, axis=1) for r in spread_rows], axis=0)
        summed = dot_nt(rows.astype(BF16), jnp.concatenate(onehot, axis=1))
        summed = summed[:72] + summed[72:]
        for cd in range(9):
            tile_grad[pl.ds(cd * COVER * TILES + t, COVER, stride=TILES), :] = summed[
                8 * cd : 8 * cd + 8
            ]
        return carry

    lax.fori_loop(0, TILES, scatter_tile, 0, unroll=UNROLL_SCATTER)

    entry_rows = entry_of(cover_rows_ref[...], u)
    entry_rows = jnp.concatenate([entry_rows[n : n + 1] for n in range(COVER)], axis=1)
    entry_ids = lax.broadcasted_iota(jnp.int32, (WIN * CAP, TILES * COVER), 0)
    pick = jnp.where(entry_ids == entry_rows, 1.0, 0.0).astype(BF16)
    for cd in range(9):
        values = tile_grad[pl.ds(cd * COVER * TILES, COVER * TILES), :]
        high = values.astype(BF16)
        low = (values - high.astype(F32)).astype(BF16)
        both = jnp.dot(
            pick, jnp.concatenate([high, low], axis=1), preferred_element_type=F32
        )
        entry_grad[pl.ds(cd * WIN * CAP, WIN * CAP), :] = both[:, :LANES] + both[:, LANES:]

    for j in range(WIN):
        rows = [[] for _ in range(3)]
        onehot = []
        for c in range(3):
            for s in range(CAP):
                ids = corner_id[pl.ds(j * 16 + c * CAP + s, 1), :]
                mine = jnp.broadcast_to(ids >> 7, (8, LANES)) == sub8
                onehot.append(lane_onehot(ids & (LANES - 1), ids16))
                for d in range(3):
                    at = (3 * c + d) * WIN * CAP + j * CAP + s
                    grad = jnp.broadcast_to(entry_grad[pl.ds(at, 1), :], (8, LANES))
                    rows[d].append(jnp.where(mine, grad, 0.0))
        stacked = jnp.concatenate([jnp.concatenate(r, axis=1) for r in rows], axis=0)
        summed = dot_nt(high_low(stacked), jnp.concatenate(onehot, axis=1))
        out_ref[j] = summed[:24] + summed[24:]


def call(kernel, out_shapes, args, scalars=0, scratch=(), name=None):
    shapes = [jax.ShapeDtypeStruct(s, F32) for s in out_shapes]
    single = len(shapes) == 1
    return pl.pallas_call(
        kernel,
        out_shape=shapes[0] if single else shapes,
        in_specs=[SMEM] * scalars + [VMEM] * (len(args) - scalars),
        out_specs=VMEM if single else [VMEM] * len(shapes),
        scratch_shapes=list(scratch),
        name=name,
    )(*args)


def exchange(array, axis):
    return lax.all_to_all(array, axis, 0, 0, tiled=True)


def tile_call(u, fetch_list, tile_cover, table, pix_slot, barycentric, camera, target):
    return call(
        tile_kernel,
        [(WIN, 24, LANES), (8, LANES)],
        (
            u.reshape(1),
            fetch_list,
            tile_cover,
            tile_cover,
            table,
            pix_slot,
            barycentric,
            camera,
            target,
        ),
        scalars=3,
        scratch=(
            pltpu.VMEM((2 * TILES, LANES), jnp.int32),
            pltpu.VMEM((16 * WIN, LANES), jnp.int32),
            pltpu.VMEM((8 * WIN * CAP, LANES), F32),
            pltpu.VMEM((WIN * CAP, LANES), F32),
            pltpu.VMEM((8 * TILES, LANES), F32),
            pltpu.VMEM((9 * 2 * TILES, LANES), F32),
            pltpu.VMEM((18 * 2 * TILES, LANES), F32),
            pltpu.VMEM((9 * TILES * COVER, LANES), F32),
            pltpu.VMEM((9 * WIN * CAP, LANES), F32),
        ),
        name="tiles",
    )


def to_all(array, axis):
    size = lax.axis_size(axis)
    return exchange(jnp.broadcast_to(array[None], (size, *array.shape)), axis)


def along_window(array, sign):
    holders = lax.axis_size("vertex")
    pairs = [
        (h * VIEWS + j, (h + sign * OFFSETS[j]) % holders * VIEWS + j)
        for h in range(holders)
        for j in range(VIEWS)
    ]
    return lax.ppermute(array, ("vertex", "view"), pairs)


def per_device(
    coeffs,
    shape_basis,
    rest_pose,
    triangles,
    fetch_list,
    tile_cover,
    pix_slot,
    barycentric,
    camera,
    target,
):
    u = lax.axis_index("vertex").astype(jnp.int32)
    pixels = (
        tile_cover.shape[0] * pix_slot.shape[1] * lax.axis_size("vertex") * lax.axis_size("view")
    )
    shapes = coeffs.shape[0]
    basis = jnp.transpose(shape_basis, (1, 0, 2))
    partial = lax.dot_general(
        coeffs[None], basis, (((1,), (1,)), ((), ())), preferred_element_type=F32
    )
    rest = rest_pose.reshape(24, LANES)
    corners = triangles.reshape(3 * BLOCKS, LANES).astype(F32)
    u, partial, rest, corners = lax.optimization_barrier((u, partial, rest, corners))
    positions = rest + to_all(partial.reshape(24, LANES), "view").sum(axis=0)
    shard = along_window(jnp.concatenate([positions, corners], axis=0), -1)
    table = to_all(shard, "view")
    parts, energy = tile_call(
        u,
        jnp.transpose(fetch_list[0]),
        jnp.transpose(tile_cover),
        table,
        pix_slot,
        jnp.transpose(barycentric, (1, 0, 2)),
        jnp.transpose(camera),
        jnp.transpose(target, (1, 0, 2)),
    )
    returned = along_window(exchange(parts, "view").sum(axis=0), 1)
    total = to_all(jnp.concatenate([returned, energy], axis=0), "view").sum(axis=0)
    vertex_grad = total[:24].reshape(3, VIEWS * LANES)
    coeff_part = jnp.sum(basis.astype(F32) * vertex_grad[:, None, :], axis=(0, 2))
    energy_part = total[24:].sum(axis=0)
    energy_part = energy_part[:shapes] + energy_part[shapes:]
    rows = jnp.concatenate([coeff_part, energy_part]).reshape(1, 2 * shapes)
    total = to_all(rows, "vertex").sum(axis=(0, 1))
    return (jnp.sum(total[shapes:]) / pixels, vertex_grad, total[:shapes])


def solution(mesh):
    placed = (
        P("view"),
        P("view", None, "vertex"),
        P(None, "vertex"),
        P(None, "vertex"),
        P(("vertex", "view"), None, None),
        P(("vertex", "view"), None),
        P(("vertex", "view"), None),
        P(("vertex", "view"), None, None),
        P(("vertex", "view"), None),
        P(("vertex", "view"), None, None),
    )
    return jax.shard_map(
        per_device,
        mesh=mesh,
        in_specs=placed,
        out_specs=(P(), P(None, "vertex"), P("view")),
        check_vma=False,
    )
```

```python
import jax
import jax.numpy as jnp
from jax import lax
from jax.experimental import pallas as pl
from jax.experimental.pallas import tpu as pltpu
from jax.sharding import PartitionSpec as P

LANES = 128
SMOOTH = 0.1
VIEWS = 8
HOLDERS = 64
UNROLL_GATHER = 32
UNROLL_SCATTER = 32
OFFSETS = (-3, -2, -1, 0, 1, 2, 3, 32)
WIN = len(OFFSETS)
CAP = 4
COVER = 8
TILES = 32
BLOCKS = 16
SHARD = 24 + 3 * BLOCKS

F32 = jnp.float32
BF16 = jnp.bfloat16
VMEM = pl.BlockSpec(memory_space=pltpu.VMEM)
SMEM = pl.BlockSpec(memory_space=pltpu.SMEM)


def pick_lanes(source, lane):
    return jnp.take_along_axis(source, lane, axis=1, mode="promise_in_bounds")


def high_low(values):
    high = values.astype(BF16).astype(F32)
    return jnp.concatenate([high, values - high], axis=0).astype(BF16)


def lane_onehot(lane_row, ids):
    row = jnp.broadcast_to(lane_row.astype(F32), (16, LANES)).astype(BF16)
    one = jnp.ones((16, LANES), BF16)
    zero = jnp.zeros((16, LANES), BF16)
    return jnp.concatenate([jnp.where(i == row, one, zero) for i in ids], axis=0)


def dot_nt(a, b):
    return lax.dot_general(a, b, (((1,), (1,)), ((), ())), preferred_element_type=F32)


def entry_of(cover, u):
    relative = ((cover >> 2) - u + 3) & (HOLDERS - 1)
    return jnp.minimum(relative, WIN - 1) * CAP + (cover & (CAP - 1))


def tile_kernel(
    u_ref,
    fetch_rows_ref,
    cover_rows_ref,
    cover_line_ref,
    table_ref,
    slot_ref,
    weight_ref,
    camera_ref,
    target_ref,
    out_ref,
    energy_ref,
    fetch_ref,
    entry_ref,
    entry_rows,
    sems,
    slot_rows,
    corner_id,
    entry_table,
    last_table,
    tile_last,
    corner_pix,
    last_pix,
    grad_pix,
    tile_grad,
    entry_grad,
):
    u = u_ref[0]
    fetch_copy = pltpu.make_async_copy(fetch_rows_ref, fetch_ref, sems.at[0])
    fetch_copy.start()
    entry_rows[...] = entry_of(cover_rows_ref[...], u) * 8
    entry_copy = pltpu.make_async_copy(entry_rows, entry_ref, sems.at[1])
    entry_copy.start()
    sub8 = lax.broadcasted_iota(jnp.int32, (8, LANES), 0)
    sub16 = lax.broadcasted_iota(jnp.int32, (16, LANES), 0)
    ids16 = [(sub16 + 16 * i).astype(F32).astype(BF16) for i in range(8)]
    for half in range(2):
        slot_rows[half * TILES : (half + 1) * TILES, :] = slot_ref[
            :, half * LANES : (half + 1) * LANES
        ]
    fetch_copy.wait()
    for j in range(WIN):
        for s in range(CAP):
            block = fetch_ref[s, (u + OFFSETS[j]) & (HOLDERS - 1)]
            for c in range(3):
                ids = table_ref[j, pl.ds(24 + c * BLOCKS + block, 1), :]
                corner_id[pl.ds(j * 16 + c * CAP + s, 1), :] = ids.astype(jnp.int32)
    for j in range(WIN):
        ids = [corner_id[pl.ds(j * 16 + 8 * i, 8), :] for i in range(2)]
        lane = [i & (LANES - 1) for i in ids]
        sub = [i >> 7 for i in ids]
        for d in range(3):
            found = [jnp.zeros((8, LANES), F32)] * 2
            for s in range(8):
                source = jnp.broadcast_to(
                    table_ref[j, 8 * d + s : 8 * d + s + 1, :], (8, LANES)
                )
                for i in range(2):
                    found[i] = jnp.where(sub[i] == s, pick_lanes(source, lane[i]), found[i])
            for c in range(3):
                rows = found[c // 2][(c % 2) * CAP : (c % 2) * CAP + CAP]
                if 3 * c + d < 8:
                    entry_table[pl.ds(j * 32 + 3 * c + d, CAP, stride=8), :] = rows
                else:
                    last_table[pl.ds(j * 32, CAP, stride=8), :] = rows

    entry_copy.wait()

    def gather_tile(t, carry):
        entries = [entry_ref[n, t] for n in range(COVER)]
        base = pl.multiple_of(t * 8, 8)
        for n in range(COVER):
            tile_last[pl.ds(base + n, 1), :] = last_table[pl.ds(entries[n], 1), :]
        last = tile_last[pl.ds(base, 8), :]
        for half in range(2):
            q = slot_rows[pl.ds(half * TILES + t, 1), :]
            q = jnp.broadcast_to(q, (8, LANES))
            lane = q & (LANES - 1)
            which = q >> 7
            first = jnp.zeros((8, LANES), F32)
            for n in range(COVER):
                at = pl.multiple_of(entries[n], 8)
                picked = pick_lanes(entry_table[pl.ds(at, 8), :], lane)
                first = jnp.where(which == n, picked, first)
            second = jnp.where(which == sub8, pick_lanes(last, lane), 0.0)
            row = half * TILES + t
            corner_pix[pl.ds(pl.multiple_of(row * 8, 8), 8), :] = first
            last_pix[pl.ds(row, 1), :] = jnp.sum(second, axis=0, keepdims=True)
        return carry

    lax.fori_loop(0, TILES, gather_tile, 0, unroll=UNROLL_GATHER)

    camera = camera_ref[...]
    energy = jnp.zeros((TILES, LANES), F32)
    for half in range(2):
        cols = slice(half * LANES, (half + 1) * LANES)
        weights = [weight_ref[c, :, cols] for c in range(3)]

        def rows_of(cd):
            return pl.ds(cd * 2 * TILES + half * TILES, TILES)

        def corner(cd):
            if cd == 8:
                return last_pix[half * TILES : (half + 1) * TILES, :]
            return corner_pix[pl.ds(half * TILES * 8 + cd, TILES, stride=8), :]

        surface = []
        for d in range(3):
            value = weights[0] * corner(d) + weights[1] * corner(3 + d)
            surface.append(value + weights[2] * corner(6 + d))
        grad_surface = [jnp.zeros((TILES, LANES), F32)] * 3
        for r in range(3):
            matrix = [camera[:, 3 * r + d : 3 * r + d + 1] for d in range(3)]
            linear = matrix[0] * surface[0]
            linear = linear + matrix[1] * surface[1]
            linear = linear + matrix[2] * surface[2]
            shaded = jnp.tanh(linear + camera[:, 9 + r : 10 + r])
            differ = shaded - target_ref[r, :, cols]
            square = differ * differ + SMOOTH * SMOOTH
            inverse = lax.rsqrt(square)
            energy = energy + square * inverse
            grad_linear = differ * inverse * (1.0 - shaded * shaded)
            for d in range(3):
                grad_surface[d] = grad_surface[d] + matrix[d] * grad_linear
        for c in range(3):
            for d in range(3):
                grad = weights[c] * grad_surface[d]
                high = grad.astype(BF16).astype(F32)
                grad_pix[rows_of(3 * c + d), :] = high
                grad_pix[rows_of(9 + 3 * c + d), :] = grad - high
    energy_ref[...] = energy[0:8] + energy[8:16] + energy[16:24] + energy[24:32]

    def scatter_tile(t, carry):
        spread_rows = [[] for _ in range(18)]
        onehot = []
        for half in range(2):
            q = slot_rows[pl.ds(half * TILES + t, 1), :]
            mine = jnp.broadcast_to(q >> 7, (8, LANES)) == sub8
            onehot.append(lane_onehot(q & (LANES - 1), ids16))
            for cd in range(18):
                grad = grad_pix[pl.ds(cd * 2 * TILES + half * TILES + t, 1), :]
                grad = jnp.broadcast_to(grad, (8, LANES))
                spread_rows[cd].append(jnp.where(mine, grad, 0.0))
        rows = jnp.concatenate([jnp.concatenate(r, axis=1) for r in spread_rows], axis=0)
        summed = dot_nt(rows.astype(BF16), jnp.concatenate(onehot, axis=1))
        summed = summed[:72] + summed[72:]
        for cd in range(9):
            at = pl.multiple_of(cd * COVER * TILES + t * COVER, COVER)
            tile_grad[pl.ds(at, COVER), :] = summed[8 * cd : 8 * cd + 8]
        return carry

    lax.fori_loop(0, TILES, scatter_tile, 0, unroll=UNROLL_SCATTER)

    entry_line = entry_of(cover_line_ref[...], u)
    entry_ids = lax.broadcasted_iota(jnp.int32, (WIN * CAP, TILES * COVER), 0)
    pick = jnp.where(entry_ids == entry_line, 1.0, 0.0).astype(BF16)
    for cd in range(9):
        values = tile_grad[pl.ds(cd * COVER * TILES, COVER * TILES), :]
        high = values.astype(BF16)
        low = (values - high.astype(F32)).astype(BF16)
        both = jnp.dot(
            pick, jnp.concatenate([high, low], axis=1), preferred_element_type=F32
        )
        entry_grad[pl.ds(cd * WIN * CAP, WIN * CAP), :] = both[:, :LANES] + both[:, LANES:]

    for j in range(WIN):
        rows = [[] for _ in range(3)]
        onehot = []
        for c in range(3):
            for s in range(CAP):
                ids = corner_id[pl.ds(j * 16 + c * CAP + s, 1), :]
                mine = jnp.broadcast_to(ids >> 7, (8, LANES)) == sub8
                onehot.append(lane_onehot(ids & (LANES - 1), ids16))
                for d in range(3):
                    at = (3 * c + d) * WIN * CAP + j * CAP + s
                    grad = jnp.broadcast_to(entry_grad[pl.ds(at, 1), :], (8, LANES))
                    rows[d].append(jnp.where(mine, grad, 0.0))
        stacked = jnp.concatenate([jnp.concatenate(r, axis=1) for r in rows], axis=0)
        summed = dot_nt(high_low(stacked), jnp.concatenate(onehot, axis=1))
        out_ref[j] = summed[:24] + summed[24:]


def call(kernel, out_shapes, args, scalars=0, scratch=(), name=None):
    args = args[:scalars] + tuple(
        pltpu.with_memory_space_constraint(a, pltpu.VMEM) for a in args[scalars:]
    )
    shapes = [pltpu.VMEM(s, F32) for s in out_shapes]
    single = len(shapes) == 1
    return pl.pallas_call(
        kernel,
        out_shape=shapes[0] if single else shapes,
        in_specs=[SMEM] * scalars + [VMEM] * (len(args) - scalars),
        out_specs=VMEM if single else [VMEM] * len(shapes),
        scratch_shapes=list(scratch),
        name=name,
    )(*args)


def exchange(array, axis):
    return lax.all_to_all(array, axis, 0, 0, tiled=True)


def tile_call(u, requests, tile_cover, cover_line, table, pix_slot, barycentric, camera, target):
    return call(
        tile_kernel,
        [(WIN, 24, LANES), (8, LANES)],
        (
            u.reshape(1),
            requests,
            jnp.transpose(tile_cover),
            cover_line,
            table,
            pix_slot,
            barycentric,
            camera,
            target,
        ),
        scalars=1,
        scratch=(
            pltpu.SMEM((CAP, HOLDERS), jnp.int32),
            pltpu.SMEM((COVER, TILES), jnp.int32),
            pltpu.VMEM((COVER, TILES), jnp.int32),
            pltpu.SemaphoreType.DMA((2,)),
            pltpu.VMEM((2 * TILES, LANES), jnp.int32),
            pltpu.VMEM((16 * WIN, LANES), jnp.int32),
            pltpu.VMEM((8 * WIN * CAP, LANES), F32),
            pltpu.VMEM((8 * WIN * CAP, LANES), F32),
            pltpu.VMEM((8 * TILES, LANES), F32),
            pltpu.VMEM((8 * 2 * TILES, LANES), F32),
            pltpu.VMEM((2 * TILES, LANES), F32),
            pltpu.VMEM((18 * 2 * TILES, LANES), F32),
            pltpu.VMEM((9 * TILES * COVER, LANES), F32),
            pltpu.VMEM((9 * WIN * CAP, LANES), F32),
        ),
        name="tiles",
    )


def to_all(array, axis):
    size = lax.axis_size(axis)
    return exchange(jnp.broadcast_to(array[None], (size, *array.shape)), axis)


def along_window(array, sign):
    holders = lax.axis_size("vertex")
    pairs = [
        (h * VIEWS + j, (h + sign * OFFSETS[j]) % holders * VIEWS + j)
        for h in range(holders)
        for j in range(VIEWS)
    ]
    return lax.ppermute(array, ("vertex", "view"), pairs)


def per_device(
    coeffs,
    shape_basis,
    rest_pose,
    triangles,
    fetch_list,
    tile_cover,
    pix_slot,
    barycentric,
    camera,
    target,
):
    u = lax.axis_index("vertex").astype(jnp.int32)
    pixels = (
        tile_cover.shape[0] * pix_slot.shape[1] * lax.axis_size("vertex") * lax.axis_size("view")
    )
    shapes = coeffs.shape[0]
    basis = jnp.transpose(shape_basis, (1, 0, 2))
    rest = rest_pose.reshape(24, LANES)
    corners = triangles.reshape(3 * BLOCKS, LANES).astype(F32)
    u, coeffs, rest, corners = lax.optimization_barrier((u, coeffs, rest, corners))
    partial = lax.dot_general(
        coeffs[None], basis, (((1,), (1,)), ((), ())), preferred_element_type=F32
    )
    partial = lax.optimization_barrier(partial)
    positions = rest + to_all(partial.reshape(24, LANES), "view").sum(axis=0)
    shard = along_window(jnp.concatenate([positions, corners], axis=0), -1)
    cover_line = tile_cover.reshape(1, TILES * COVER)
    requests = jnp.maximum(jnp.transpose(fetch_list[0]), 0)
    shard, cover_line, requests, camera = lax.optimization_barrier(
        (shard, cover_line, requests, camera)
    )
    table = to_all(shard, "view")
    parts, energy = tile_call(
        u,
        requests,
        tile_cover,
        cover_line,
        table,
        pix_slot,
        jnp.transpose(barycentric, (1, 0, 2)),
        camera,
        jnp.transpose(target, (1, 0, 2)),
    )
    returned = along_window(exchange(parts, "view").sum(axis=0), 1)
    total = to_all(jnp.concatenate([returned, energy], axis=0), "view").sum(axis=0)
    vertex_grad = total[:24].reshape(3, VIEWS * LANES)
    coeff_part = jnp.sum(basis.astype(F32) * vertex_grad[:, None, :], axis=(0, 2))
    energy_part = total[24:].sum(axis=0)
    energy_part = energy_part[:shapes] + energy_part[shapes:]
    rows = jnp.concatenate([coeff_part, energy_part]).reshape(1, 2 * shapes)
    total = to_all(rows, "vertex").sum(axis=(0, 1))
    total, vertex_grad = lax.optimization_barrier((total, vertex_grad))
    return (jnp.sum(total[shapes:]) / pixels, vertex_grad, total[:shapes])


def solution(mesh):
    placed = (
        P("view"),
        P("view", None, "vertex"),
        P(None, "vertex"),
        P(None, "vertex"),
        P(("vertex", "view"), None, None),
        P(("vertex", "view"), None),
        P(("vertex", "view"), None),
        P(("vertex", "view"), None, None),
        P(("vertex", "view"), None),
        P(("vertex", "view"), None, None),
    )
    return jax.shard_map(
        per_device,
        mesh=mesh,
        in_specs=placed,
        out_specs=(P(), P(None, "vertex"), P("view")),
        check_vma=False,
    )
```

```python
import jax
import jax.numpy as jnp
from jax import lax
from jax.experimental import pallas as pl
from jax.experimental.pallas import tpu as pltpu
from jax.sharding import PartitionSpec as P

LANES = 128
SMOOTH = 0.1
VIEWS = 8
HOLDERS = 64
UNROLL_GATHER = 32
UNROLL_SCATTER = 32
OFFSETS = (-3, -2, -1, 0, 1, 2, 3, 32)
WIN = len(OFFSETS)
CAP = 4
COVER = 8
TILES = 32
BLOCKS = 16
SHARD = 24 + 3 * BLOCKS

F32 = jnp.float32
BF16 = jnp.bfloat16
VMEM = pl.BlockSpec(memory_space=pltpu.VMEM)
SMEM = pl.BlockSpec(memory_space=pltpu.SMEM)


def pick_lanes(source, lane):
    return jnp.take_along_axis(source, lane, axis=1, mode="promise_in_bounds")


def offset_kernel(coeff_ref, basis_ref, rest_ref, corner_ref, out_ref, shard_ref):
    coeffs = jnp.broadcast_to(coeff_ref[...].astype(F32), (16, coeff_ref.shape[1])).astype(BF16)
    for d in range(3):
        row = jnp.dot(coeffs, basis_ref[d], preferred_element_type=F32)[0:1]
        for s in range(8):
            cols = slice(s * LANES, (s + 1) * LANES)
            for v in range(VIEWS):
                out_ref[v, 8 * d + s : 8 * d + s + 1, :] = row[:, cols]
            shard_ref[8 * d + s : 8 * d + s + 1, :] = rest_ref[d : d + 1, cols]
    for c in range(3):
        for b in range(BLOCKS):
            shard_ref[24 + c * BLOCKS + b : 25 + c * BLOCKS + b, :] = corner_ref[
                c : c + 1, b * LANES : (b + 1) * LANES
            ].astype(F32)


def finish_kernel(pixels_ref, total_ref, grad_ref, coeff_ref, loss_ref, out_ref):
    shapes = coeff_ref.shape[1]
    coeff_ref[...] = total_ref[:, :shapes]
    loss_ref[...] = jnp.sum(total_ref[:, shapes:], axis=1, keepdims=True) * pixels_ref[0]
    out_ref[...] = grad_ref[...]


def lane_onehot(lane_row, ids):
    row = jnp.broadcast_to(lane_row.astype(F32), (16, LANES)).astype(BF16)
    one = jnp.ones((16, LANES), BF16)
    zero = jnp.zeros((16, LANES), BF16)
    return jnp.concatenate([jnp.where(i == row, one, zero) for i in ids], axis=0)


def dot_nt(a, b):
    return lax.dot_general(a, b, (((1,), (1,)), ((), ())), preferred_element_type=F32)


def entry_of(cover, u):
    relative = ((cover >> 2) - u + 3) & (HOLDERS - 1)
    return jnp.minimum(relative, WIN - 1) * CAP + (cover & (CAP - 1))


def tile_kernel(
    u_ref,
    fetch_rows_ref,
    cover_rows_ref,
    cover_line_ref,
    table_ref,
    slot_ref,
    weight_ref,
    camera_ref,
    target_ref,
    out_ref,
    energy_ref,
    fetch_ref,
    entry_ref,
    entry_rows,
    sems,
    slot_rows,
    corner_id,
    entry_table,
    last_table,
    tile_last,
    corner_pix,
    last_pix,
    grad_pix,
    tile_grad,
    entry_grad,
):
    u = u_ref[0]
    fetch_copy = pltpu.make_async_copy(fetch_rows_ref, fetch_ref, sems.at[0])
    fetch_copy.start()
    entry_rows[...] = entry_of(cover_rows_ref[...], u) * 8
    entry_copy = pltpu.make_async_copy(entry_rows, entry_ref, sems.at[1])
    entry_copy.start()
    sub8 = lax.broadcasted_iota(jnp.int32, (8, LANES), 0)
    sub16 = lax.broadcasted_iota(jnp.int32, (16, LANES), 0)
    ids16 = [(sub16 + 16 * i).astype(F32).astype(BF16) for i in range(8)]
    for half in range(2):
        slot_rows[half * TILES : (half + 1) * TILES, :] = slot_ref[
            :, half * LANES : (half + 1) * LANES
        ]
    fetch_copy.wait()
    for j in range(WIN):
        for s in range(CAP):
            block = fetch_ref[s, (u + OFFSETS[j]) & (HOLDERS - 1)]
            for c in range(3):
                ids = table_ref[j, pl.ds(24 + c * BLOCKS + block, 1), :]
                corner_id[pl.ds(j * 16 + c * CAP + s, 1), :] = ids.astype(jnp.int32)
    for j in range(WIN):
        ids = [corner_id[pl.ds(j * 16 + 8 * i, 8), :] for i in range(2)]
        lane = [i & (LANES - 1) for i in ids]
        sub = [i >> 7 for i in ids]
        for d in range(3):
            found = [jnp.zeros((8, LANES), F32)] * 2
            for s in range(8):
                source = jnp.broadcast_to(
                    table_ref[j, 8 * d + s : 8 * d + s + 1, :], (8, LANES)
                )
                for i in range(2):
                    found[i] = jnp.where(sub[i] == s, pick_lanes(source, lane[i]), found[i])
            for c in range(3):
                rows = found[c // 2][(c % 2) * CAP : (c % 2) * CAP + CAP]
                if 3 * c + d < 8:
                    entry_table[pl.ds(j * 32 + 3 * c + d, CAP, stride=8), :] = rows
                else:
                    last_table[pl.ds(j * 32, CAP, stride=8), :] = rows

    entry_copy.wait()

    def gather_tile(t, carry):
        entries = [entry_ref[n, t] for n in range(COVER)]
        base = pl.multiple_of(t * 8, 8)
        for n in range(COVER):
            tile_last[pl.ds(base + n, 1), :] = last_table[pl.ds(entries[n], 1), :]
        last = tile_last[pl.ds(base, 8), :]
        for half in range(2):
            q = slot_rows[pl.ds(half * TILES + t, 1), :]
            q = jnp.broadcast_to(q, (8, LANES))
            lane = q & (LANES - 1)
            which = q >> 7
            first = jnp.zeros((8, LANES), F32)
            for n in range(COVER):
                at = pl.multiple_of(entries[n], 8)
                picked = pick_lanes(entry_table[pl.ds(at, 8), :], lane)
                first = jnp.where(which == n, picked, first)
            second = jnp.where(which == sub8, pick_lanes(last, lane), 0.0)
            row = half * TILES + t
            corner_pix[pl.ds(pl.multiple_of(row * 8, 8), 8), :] = first
            last_pix[pl.ds(row, 1), :] = jnp.sum(second, axis=0, keepdims=True)
        return carry

    lax.fori_loop(0, TILES, gather_tile, 0, unroll=UNROLL_GATHER)

    camera = camera_ref[...].T
    energy = jnp.zeros((TILES, LANES), F32)
    for half in range(2):
        cols = slice(half * LANES, (half + 1) * LANES)
        weights = [weight_ref[c, :, cols] for c in range(3)]

        def rows_of(cd):
            return pl.ds(cd * 2 * TILES + half * TILES, TILES)

        def corner(cd):
            if cd == 8:
                return last_pix[half * TILES : (half + 1) * TILES, :]
            return corner_pix[pl.ds(half * TILES * 8 + cd, TILES, stride=8), :]

        surface = []
        for d in range(3):
            value = weights[0] * corner(d) + weights[1] * corner(3 + d)
            surface.append(value + weights[2] * corner(6 + d))
        grad_surface = [jnp.zeros((TILES, LANES), F32)] * 3
        for r in range(3):
            matrix = [camera[:, 3 * r + d : 3 * r + d + 1] for d in range(3)]
            linear = matrix[0] * surface[0]
            linear = linear + matrix[1] * surface[1]
            linear = linear + matrix[2] * surface[2]
            shaded = jnp.tanh(linear + camera[:, 9 + r : 10 + r])
            differ = shaded - target_ref[r, :, cols]
            square = differ * differ + SMOOTH * SMOOTH
            inverse = lax.rsqrt(square)
            energy = energy + square * inverse
            grad_linear = differ * inverse * (1.0 - shaded * shaded)
            for d in range(3):
                grad_surface[d] = grad_surface[d] + matrix[d] * grad_linear
        for c in range(3):
            for d in range(3):
                grad = weights[c] * grad_surface[d]
                high = grad.astype(BF16).astype(F32)
                grad_pix[rows_of(3 * c + d), :] = high
                grad_pix[rows_of(9 + 3 * c + d), :] = grad - high
    energy_ref[...] = energy[0:8] + energy[8:16] + energy[16:24] + energy[24:32]

    def scatter_tile(t, carry):
        spread_rows = [[] for _ in range(18)]
        onehot = []
        for half in range(2):
            q = slot_rows[pl.ds(half * TILES + t, 1), :]
            mine = jnp.broadcast_to(q >> 7, (8, LANES)) == sub8
            onehot.append(lane_onehot(q & (LANES - 1), ids16))
            for cd in range(18):
                grad = grad_pix[pl.ds(cd * 2 * TILES + half * TILES + t, 1), :]
                grad = jnp.broadcast_to(grad, (8, LANES))
                spread_rows[cd].append(jnp.where(mine, grad, 0.0))
        rows = jnp.concatenate([jnp.concatenate(r, axis=1) for r in spread_rows], axis=0)
        summed = dot_nt(rows.astype(BF16), jnp.concatenate(onehot, axis=1))
        summed = summed[:72] + summed[72:]
        for cd in range(9):
            at = pl.multiple_of(cd * COVER * TILES + t * COVER, COVER)
            tile_grad[pl.ds(at, COVER), :] = summed[8 * cd : 8 * cd + 8]
        return carry

    lax.fori_loop(0, TILES, scatter_tile, 0, unroll=UNROLL_SCATTER)

    entry_line = entry_of(cover_line_ref[...], u)
    entry_ids = lax.broadcasted_iota(jnp.int32, (WIN * CAP, TILES * COVER), 0)
    pick = jnp.where(entry_ids == entry_line, 1.0, 0.0).astype(BF16)
    for cd in range(9):
        values = tile_grad[pl.ds(cd * COVER * TILES, COVER * TILES), :]
        high = values.astype(BF16)
        low = (values - high.astype(F32)).astype(BF16)
        both = jnp.dot(
            pick, jnp.concatenate([high, low], axis=1), preferred_element_type=F32
        )
        both = both[:, :LANES] + both[:, LANES:]
        high = both.astype(BF16).astype(F32)
        entry_grad[pl.ds(cd * WIN * CAP, WIN * CAP), :] = high
        entry_grad[pl.ds((9 + cd) * WIN * CAP, WIN * CAP), :] = both - high

    for j in range(WIN):
        rows = [[] for _ in range(6)]
        onehot = []
        for c in range(3):
            for s in range(CAP):
                ids = corner_id[pl.ds(j * 16 + c * CAP + s, 1), :]
                mine = jnp.broadcast_to(ids >> 7, (8, LANES)) == sub8
                onehot.append(lane_onehot(ids & (LANES - 1), ids16))
                for d in range(6):
                    at = (9 * (d // 3) + 3 * c + d % 3) * WIN * CAP + j * CAP + s
                    grad = jnp.broadcast_to(entry_grad[pl.ds(at, 1), :], (8, LANES))
                    rows[d].append(jnp.where(mine, grad, 0.0))
        stacked = jnp.concatenate([jnp.concatenate(r, axis=1) for r in rows], axis=0)
        summed = dot_nt(stacked.astype(BF16), jnp.concatenate(onehot, axis=1))
        out_ref[j] = summed[:24] + summed[24:]


def call(kernel, out_shapes, args, scalars=0, scratch=(), name=None, pinned=(True, True)):
    if pinned[0]:
        args = args[:scalars] + tuple(
            pltpu.with_memory_space_constraint(a, pltpu.VMEM) for a in args[scalars:]
        )
    kind = pltpu.VMEM if pinned[1] else jax.ShapeDtypeStruct
    return pl.pallas_call(
        kernel,
        out_shape=[kind(s, F32) for s in out_shapes],
        in_specs=[SMEM] * scalars + [VMEM] * (len(args) - scalars),
        out_specs=[VMEM] * len(out_shapes),
        scratch_shapes=list(scratch),
        name=name,
    )(*args)


def exchange(array, axis):
    return lax.all_to_all(array, axis, 0, 0, tiled=True)


def tile_call(u, requests, tile_cover, cover_line, table, pix_slot, barycentric, camera, target):
    return call(
        tile_kernel,
        [(WIN, 24, LANES), (8, LANES)],
        (
            u.reshape(1),
            requests,
            jnp.transpose(tile_cover),
            cover_line,
            table,
            pix_slot,
            barycentric,
            camera,
            target,
        ),
        scalars=1,
        scratch=(
            pltpu.SMEM((CAP, HOLDERS), jnp.int32),
            pltpu.SMEM((COVER, TILES), jnp.int32),
            pltpu.VMEM((COVER, TILES), jnp.int32),
            pltpu.SemaphoreType.DMA((2,)),
            pltpu.VMEM((2 * TILES, LANES), jnp.int32),
            pltpu.VMEM((16 * WIN, LANES), jnp.int32),
            pltpu.VMEM((8 * WIN * CAP, LANES), F32),
            pltpu.VMEM((8 * WIN * CAP, LANES), F32),
            pltpu.VMEM((8 * TILES, LANES), F32),
            pltpu.VMEM((8 * 2 * TILES, LANES), F32),
            pltpu.VMEM((2 * TILES, LANES), F32),
            pltpu.VMEM((18 * 2 * TILES, LANES), F32),
            pltpu.VMEM((9 * TILES * COVER, LANES), F32),
            pltpu.VMEM((18 * WIN * CAP, LANES), F32),
        ),
        name="tiles",
    )


def to_all(array, axis):
    size = lax.axis_size(axis)
    return exchange(jnp.broadcast_to(array[None], (size, *array.shape)), axis)


def along_window(array, sign):
    holders = lax.axis_size("vertex")
    pairs = [
        (h * VIEWS + j, (h + sign * OFFSETS[j]) % holders * VIEWS + j)
        for h in range(holders)
        for j in range(VIEWS)
    ]
    return lax.ppermute(array, ("vertex", "view"), pairs)


def per_device(
    coeffs,
    shape_basis,
    rest_pose,
    triangles,
    fetch_list,
    tile_cover,
    pix_slot,
    barycentric,
    camera,
    target,
):
    u = lax.axis_index("vertex").astype(jnp.int32)
    pixels = (
        tile_cover.shape[0] * pix_slot.shape[1] * lax.axis_size("vertex") * lax.axis_size("view")
    )
    shapes = coeffs.shape[0]
    basis = jnp.transpose(shape_basis, (1, 0, 2))
    partial, shard = call(
        offset_kernel,
        [(VIEWS, 24, LANES), (SHARD, LANES)],
        (coeffs.reshape(1, shapes), basis, rest_pose, triangles),
        name="offsets",
        pinned=(False, True),
    )
    offsets = exchange(partial, "view").sum(axis=0)
    shard = shard + jnp.pad(offsets, ((0, SHARD - 24), (0, 0)))
    shard = along_window(shard, -1)
    cover_line = tile_cover.reshape(1, TILES * COVER)
    requests = jnp.maximum(jnp.transpose(fetch_list[0]), 0)
    lens = jnp.pad(jnp.transpose(camera), ((0, 4), (0, 0)))
    shard, cover_line, requests, lens, u = lax.optimization_barrier(
        (shard, cover_line, requests, lens, u)
    )
    table = to_all(shard, "view")
    parts, energy = tile_call(
        u,
        requests,
        tile_cover,
        cover_line,
        table,
        pix_slot,
        jnp.transpose(barycentric, (1, 0, 2)),
        lens,
        jnp.transpose(target, (1, 0, 2)),
    )
    returned = along_window(exchange(parts, "view").sum(axis=0), 1)
    total = to_all(jnp.concatenate([returned, energy], axis=0), "view").sum(axis=0)
    vertex_grad = total[:24].reshape(3, VIEWS * LANES)
    coeff_part = jnp.sum(basis.astype(F32) * vertex_grad[:, None, :], axis=(0, 2))
    energy_part = total[24:].sum(axis=0)
    energy_part = energy_part[:shapes] + energy_part[shapes:]
    rows = jnp.concatenate([coeff_part, energy_part]).reshape(1, 2 * shapes)
    total = to_all(rows, "vertex").sum(axis=0)
    coeff_grad, loss, vertex_grad = call(
        finish_kernel,
        [(1, shapes), (1, 1), vertex_grad.shape],
        (jnp.full((1,), 1.0 / pixels, F32), total, vertex_grad),
        scalars=1,
        name="finish",
        pinned=(True, False),
    )
    return (loss.reshape(()), vertex_grad, coeff_grad.reshape(shapes))


def solution(mesh):
    placed = (
        P("view"),
        P("view", None, "vertex"),
        P(None, "vertex"),
        P(None, "vertex"),
        P(("vertex", "view"), None, None),
        P(("vertex", "view"), None),
        P(("vertex", "view"), None),
        P(("vertex", "view"), None, None),
        P(("vertex", "view"), None),
        P(("vertex", "view"), None, None),
    )
    return jax.shard_map(
        per_device,
        mesh=mesh,
        in_specs=placed,
        out_specs=(P(), P(None, "vertex"), P("view")),
        check_vma=False,
    )
```

```python
import jax
import jax.numpy as jnp
from jax import lax
from jax.experimental import pallas as pl
from jax.experimental.pallas import tpu as pltpu
from jax.sharding import PartitionSpec as P

LANES = 128
SMOOTH = 0.1
VIEWS = 8
HOLDERS = 64
UNROLL_GATHER = 32
UNROLL_SCATTER = 32
OFFSETS = (-3, -2, -1, 0, 1, 2, 3, 32)
WIN = len(OFFSETS)
CAP = 4
COVER = 8
TILES = 32
BLOCKS = 16
PACKED = 40
SHARD = 24 + 3 * BLOCKS

F32 = jnp.float32
BF16 = jnp.bfloat16
VMEM = pl.BlockSpec(memory_space=pltpu.VMEM)
SMEM = pl.BlockSpec(memory_space=pltpu.SMEM)


def pick_lanes(source, lane):
    return jnp.take_along_axis(source, lane, axis=1, mode="promise_in_bounds")


def offset_kernel(
    u_ref, coeff_ref, basis_ref, rest_ref, corner_ref, fetch_ref, out_ref, shard_ref
):
    requests = jnp.maximum(fetch_ref[...], 0).astype(F32)
    holder = lax.broadcasted_iota(jnp.int32, requests.shape, 1)
    for v in range(VIEWS):
        mine = holder == ((u_ref[0] + OFFSETS[v]) & (HOLDERS - 1))
        wanted = jnp.sum(jnp.where(mine, requests, 0.0), axis=1, keepdims=True)
        out_ref[v, 24:28, :] = jnp.broadcast_to(wanted, (CAP, LANES))
        out_ref[v, 28:32, :] = jnp.zeros((CAP, LANES), F32)
    coeffs = jnp.broadcast_to(coeff_ref[...].astype(F32), (16, coeff_ref.shape[1])).astype(BF16)
    for d in range(3):
        row = jnp.dot(coeffs, basis_ref[d], preferred_element_type=F32)[0:1]
        for s in range(8):
            cols = slice(s * LANES, (s + 1) * LANES)
            for v in range(VIEWS):
                out_ref[v, 8 * d + s : 8 * d + s + 1, :] = row[:, cols]
            shard_ref[8 * d + s : 8 * d + s + 1, :] = rest_ref[d : d + 1, cols]
    for c in range(3):
        for b in range(BLOCKS):
            shard_ref[24 + c * BLOCKS + b : 25 + c * BLOCKS + b, :] = corner_ref[
                c : c + 1, b * LANES : (b + 1) * LANES
            ].astype(F32)


def pack_kernel(shard_ref, parts_ref, out_ref):
    wanted = jnp.concatenate([parts_ref[v, 24:28, :BLOCKS] for v in range(VIEWS)], axis=0)
    ids = lax.broadcasted_iota(jnp.int32, wanted.shape, 1)
    pick = jnp.where(wanted.astype(jnp.int32) == ids, 1.0, 0.0)
    for v in range(VIEWS):
        out_ref[v, 0:24, :] = shard_ref[0:24, :]
        out_ref[v, 36:40, :] = jnp.zeros((CAP, LANES), F32)
    for c in range(3):
        rows = jnp.dot(
            pick,
            shard_ref[24 + c * BLOCKS : 24 + (c + 1) * BLOCKS, :],
            precision=lax.Precision.HIGHEST,
            preferred_element_type=F32,
        )
        for v in range(VIEWS):
            out_ref[v, 24 + c * CAP : 24 + (c + 1) * CAP, :] = rows[v * CAP : (v + 1) * CAP]


def finish_kernel(pixels_ref, total_ref, grad_ref, coeff_ref, loss_ref, out_ref):
    shapes = coeff_ref.shape[1]
    coeff_ref[...] = total_ref[:, :shapes]
    loss_ref[...] = jnp.sum(total_ref[:, shapes:], axis=1, keepdims=True) * pixels_ref[0]
    out_ref[...] = grad_ref[...]


def lane_onehot(lane_row, ids):
    row = jnp.broadcast_to(lane_row.astype(F32), (16, LANES)).astype(BF16)
    one = jnp.ones((16, LANES), BF16)
    zero = jnp.zeros((16, LANES), BF16)
    return jnp.concatenate([jnp.where(i == row, one, zero) for i in ids], axis=0)


def dot_nt(a, b):
    return lax.dot_general(a, b, (((1,), (1,)), ((), ())), preferred_element_type=F32)


def entry_of(cover, u):
    relative = ((cover >> 2) - u + 3) & (HOLDERS - 1)
    return jnp.minimum(relative, WIN - 1) * CAP + (cover & (CAP - 1))


def tile_kernel(
    u_ref,
    cover_rows_ref,
    cover_line_ref,
    table_ref,
    slot_ref,
    weight_ref,
    camera_ref,
    target_ref,
    out_ref,
    energy_ref,
    entry_ref,
    entry_rows,
    sems,
    slot_rows,
    corner_id,
    entry_table,
    last_table,
    tile_last,
    corner_pix,
    last_pix,
    grad_pix,
    tile_grad,
    entry_grad,
):
    u = u_ref[0]
    entry_rows[...] = entry_of(cover_rows_ref[...], u) * 8
    entry_copy = pltpu.make_async_copy(entry_rows, entry_ref, sems.at[0])
    entry_copy.start()
    sub8 = lax.broadcasted_iota(jnp.int32, (8, LANES), 0)
    sub16 = lax.broadcasted_iota(jnp.int32, (16, LANES), 0)
    ids16 = [(sub16 + 16 * i).astype(F32).astype(BF16) for i in range(8)]
    for half in range(2):
        slot_rows[half * TILES : (half + 1) * TILES, :] = slot_ref[
            :, half * LANES : (half + 1) * LANES
        ]
    for j in range(WIN):
        corner_id[j * 16 : j * 16 + 16, :] = table_ref[j, 24:40, :].astype(jnp.int32)
    for j in range(WIN):
        ids = [corner_id[pl.ds(j * 16 + 8 * i, 8), :] for i in range(2)]
        lane = [i & (LANES - 1) for i in ids]
        sub = [i >> 7 for i in ids]
        for d in range(3):
            found = [jnp.zeros((8, LANES), F32)] * 2
            for s in range(8):
                source = jnp.broadcast_to(
                    table_ref[j, 8 * d + s : 8 * d + s + 1, :], (8, LANES)
                )
                for i in range(2):
                    found[i] = jnp.where(sub[i] == s, pick_lanes(source, lane[i]), found[i])
            for c in range(3):
                rows = found[c // 2][(c % 2) * CAP : (c % 2) * CAP + CAP]
                if 3 * c + d < 8:
                    entry_table[pl.ds(j * 32 + 3 * c + d, CAP, stride=8), :] = rows
                else:
                    last_table[pl.ds(j * 32, CAP, stride=8), :] = rows

    entry_copy.wait()

    def gather_tile(t, carry):
        entries = [entry_ref[n, t] for n in range(COVER)]
        base = pl.multiple_of(t * 8, 8)
        for n in range(COVER):
            tile_last[pl.ds(base + n, 1), :] = last_table[pl.ds(entries[n], 1), :]
        last = tile_last[pl.ds(base, 8), :]
        for half in range(2):
            q = slot_rows[pl.ds(half * TILES + t, 1), :]
            q = jnp.broadcast_to(q, (8, LANES))
            lane = q & (LANES - 1)
            which = q >> 7
            first = jnp.zeros((8, LANES), F32)
            for n in range(COVER):
                at = pl.multiple_of(entries[n], 8)
                picked = pick_lanes(entry_table[pl.ds(at, 8), :], lane)
                first = jnp.where(which == n, picked, first)
            second = jnp.where(which == sub8, pick_lanes(last, lane), 0.0)
            row = half * TILES + t
            corner_pix[pl.ds(pl.multiple_of(row * 8, 8), 8), :] = first
            last_pix[pl.ds(row, 1), :] = jnp.sum(second, axis=0, keepdims=True)
        return carry

    lax.fori_loop(0, TILES, gather_tile, 0, unroll=UNROLL_GATHER)

    camera = camera_ref[...].T
    energy = jnp.zeros((TILES, LANES), F32)
    for half in range(2):
        cols = slice(half * LANES, (half + 1) * LANES)
        weights = [weight_ref[c, :, cols] for c in range(3)]

        def rows_of(cd):
            return pl.ds(cd * 2 * TILES + half * TILES, TILES)

        def corner(cd):
            if cd == 8:
                return last_pix[half * TILES : (half + 1) * TILES, :]
            return corner_pix[pl.ds(half * TILES * 8 + cd, TILES, stride=8), :]

        surface = []
        for d in range(3):
            value = weights[0] * corner(d) + weights[1] * corner(3 + d)
            surface.append(value + weights[2] * corner(6 + d))
        grad_surface = [jnp.zeros((TILES, LANES), F32)] * 3
        for r in range(3):
            matrix = [camera[:, 3 * r + d : 3 * r + d + 1] for d in range(3)]
            linear = matrix[0] * surface[0]
            linear = linear + matrix[1] * surface[1]
            linear = linear + matrix[2] * surface[2]
            shaded = jnp.tanh(linear + camera[:, 9 + r : 10 + r])
            differ = shaded - target_ref[r, :, cols]
            square = differ * differ + SMOOTH * SMOOTH
            inverse = lax.rsqrt(square)
            energy = energy + square * inverse
            grad_linear = differ * inverse * (1.0 - shaded * shaded)
            for d in range(3):
                grad_surface[d] = grad_surface[d] + matrix[d] * grad_linear
        for c in range(3):
            for d in range(3):
                grad = weights[c] * grad_surface[d]
                high = grad.astype(BF16).astype(F32)
                grad_pix[rows_of(3 * c + d), :] = high
                grad_pix[rows_of(9 + 3 * c + d), :] = grad - high
    energy_ref[...] = energy[0:8] + energy[8:16] + energy[16:24] + energy[24:32]

    def scatter_tile(t, carry):
        spread_rows = [[] for _ in range(18)]
        onehot = []
        for half in range(2):
            q = slot_rows[pl.ds(half * TILES + t, 1), :]
            mine = jnp.broadcast_to(q >> 7, (8, LANES)) == sub8
            onehot.append(lane_onehot(q & (LANES - 1), ids16))
            for cd in range(18):
                grad = grad_pix[pl.ds(cd * 2 * TILES + half * TILES + t, 1), :]
                grad = jnp.broadcast_to(grad, (8, LANES))
                spread_rows[cd].append(jnp.where(mine, grad, 0.0))
        rows = jnp.concatenate([jnp.concatenate(r, axis=1) for r in spread_rows], axis=0)
        summed = dot_nt(rows.astype(BF16), jnp.concatenate(onehot, axis=1))
        summed = summed[:72] + summed[72:]
        for cd in range(9):
            at = pl.multiple_of(cd * COVER * TILES + t * COVER, COVER)
            tile_grad[pl.ds(at, COVER), :] = summed[8 * cd : 8 * cd + 8]
        return carry

    lax.fori_loop(0, TILES, scatter_tile, 0, unroll=UNROLL_SCATTER)

    entry_line = entry_of(cover_line_ref[...], u)
    entry_ids = lax.broadcasted_iota(jnp.int32, (WIN * CAP, TILES * COVER), 0)
    pick = jnp.where(entry_ids == entry_line, 1.0, 0.0).astype(BF16)
    for cd in range(9):
        values = tile_grad[pl.ds(cd * COVER * TILES, COVER * TILES), :]
        high = values.astype(BF16)
        low = (values - high.astype(F32)).astype(BF16)
        both = jnp.dot(
            pick, jnp.concatenate([high, low], axis=1), preferred_element_type=F32
        )
        both = both[:, :LANES] + both[:, LANES:]
        high = both.astype(BF16).astype(F32)
        entry_grad[pl.ds(cd * WIN * CAP, WIN * CAP), :] = high
        entry_grad[pl.ds((9 + cd) * WIN * CAP, WIN * CAP), :] = both - high

    for j in range(WIN):
        rows = [[] for _ in range(6)]
        onehot = []
        for c in range(3):
            for s in range(CAP):
                ids = corner_id[pl.ds(j * 16 + c * CAP + s, 1), :]
                mine = jnp.broadcast_to(ids >> 7, (8, LANES)) == sub8
                onehot.append(lane_onehot(ids & (LANES - 1), ids16))
                for d in range(6):
                    at = (9 * (d // 3) + 3 * c + d % 3) * WIN * CAP + j * CAP + s
                    grad = jnp.broadcast_to(entry_grad[pl.ds(at, 1), :], (8, LANES))
                    rows[d].append(jnp.where(mine, grad, 0.0))
        stacked = jnp.concatenate([jnp.concatenate(r, axis=1) for r in rows], axis=0)
        summed = dot_nt(stacked.astype(BF16), jnp.concatenate(onehot, axis=1))
        out_ref[j] = summed[:24] + summed[24:]


def call(kernel, out_shapes, args, scalars=0, scratch=(), name=None, pinned=(True, True)):
    if pinned[0]:
        args = args[:scalars] + tuple(
            pltpu.with_memory_space_constraint(a, pltpu.VMEM) for a in args[scalars:]
        )
    kind = pltpu.VMEM if pinned[1] else jax.ShapeDtypeStruct
    return pl.pallas_call(
        kernel,
        out_shape=[kind(s, F32) for s in out_shapes],
        in_specs=[SMEM] * scalars + [VMEM] * (len(args) - scalars),
        out_specs=[VMEM] * len(out_shapes),
        scratch_shapes=list(scratch),
        name=name,
    )(*args)


def exchange(array, axis):
    return lax.all_to_all(array, axis, 0, 0, tiled=True)


def tile_call(u, tile_cover, cover_line, table, pix_slot, barycentric, camera, target):
    return call(
        tile_kernel,
        [(WIN, 24, LANES), (8, LANES)],
        (
            u.reshape(1),
            jnp.transpose(tile_cover),
            cover_line,
            table,
            pix_slot,
            barycentric,
            camera,
            target,
        ),
        scalars=1,
        scratch=(
            pltpu.SMEM((COVER, TILES), jnp.int32),
            pltpu.VMEM((COVER, TILES), jnp.int32),
            pltpu.SemaphoreType.DMA((1,)),
            pltpu.VMEM((2 * TILES, LANES), jnp.int32),
            pltpu.VMEM((16 * WIN, LANES), jnp.int32),
            pltpu.VMEM((8 * WIN * CAP, LANES), F32),
            pltpu.VMEM((8 * WIN * CAP, LANES), F32),
            pltpu.VMEM((8 * TILES, LANES), F32),
            pltpu.VMEM((8 * 2 * TILES, LANES), F32),
            pltpu.VMEM((2 * TILES, LANES), F32),
            pltpu.VMEM((18 * 2 * TILES, LANES), F32),
            pltpu.VMEM((9 * TILES * COVER, LANES), F32),
            pltpu.VMEM((18 * WIN * CAP, LANES), F32),
        ),
        name="tiles",
    )


def to_all(array, axis):
    size = lax.axis_size(axis)
    return exchange(jnp.broadcast_to(array[None], (size, *array.shape)), axis)


def along_window(array, sign):
    holders = lax.axis_size("vertex")
    pairs = [
        (h * VIEWS + j, (h + sign * OFFSETS[j]) % holders * VIEWS + j)
        for h in range(holders)
        for j in range(VIEWS)
    ]
    return lax.ppermute(array, ("vertex", "view"), pairs)


def per_device(
    coeffs,
    shape_basis,
    rest_pose,
    triangles,
    fetch_list,
    tile_cover,
    pix_slot,
    barycentric,
    camera,
    target,
):
    u = lax.axis_index("vertex").astype(jnp.int32)
    pixels = (
        tile_cover.shape[0] * pix_slot.shape[1] * lax.axis_size("vertex") * lax.axis_size("view")
    )
    shapes = coeffs.shape[0]
    basis = jnp.transpose(shape_basis, (1, 0, 2))
    partial, shard = call(
        offset_kernel,
        [(VIEWS, 32, LANES), (SHARD, LANES)],
        (
            u.reshape(1),
            coeffs.reshape(1, shapes),
            basis,
            rest_pose,
            triangles,
            jnp.transpose(fetch_list[0]),
        ),
        scalars=1,
        name="offsets",
        pinned=(False, True),
    )
    parts = exchange(partial, "view")
    offsets = parts[:, :24].sum(axis=0)
    shard = shard + jnp.pad(offsets, ((0, SHARD - 24), (0, 0)))
    shard = along_window(shard, -1)
    cover_line = tile_cover.reshape(1, TILES * COVER)
    lens = jnp.pad(jnp.transpose(camera), ((0, 4), (0, 0)))
    shard, cover_line, lens, u = lax.optimization_barrier((shard, cover_line, lens, u))
    packed = call(pack_kernel, [(VIEWS, PACKED, LANES)], (shard, parts), name="pack")[0]
    table = exchange(packed, "view")
    grads, energy = tile_call(
        u,
        tile_cover,
        cover_line,
        table,
        pix_slot,
        jnp.transpose(barycentric, (1, 0, 2)),
        lens,
        jnp.transpose(target, (1, 0, 2)),
    )
    returned = along_window(exchange(grads, "view").sum(axis=0), 1)
    total = to_all(jnp.concatenate([returned, energy], axis=0), "view").sum(axis=0)
    vertex_grad = total[:24].reshape(3, VIEWS * LANES)
    coeff_part = jnp.sum(basis.astype(F32) * vertex_grad[:, None, :], axis=(0, 2))
    energy_part = total[24:].sum(axis=0)
    energy_part = energy_part[:shapes] + energy_part[shapes:]
    rows = jnp.concatenate([coeff_part, energy_part]).reshape(1, 2 * shapes)
    total = to_all(rows, "vertex").sum(axis=0)
    coeff_grad, loss, vertex_grad = call(
        finish_kernel,
        [(1, shapes), (1, 1), vertex_grad.shape],
        (jnp.full((1,), 1.0 / pixels, F32), total, vertex_grad),
        scalars=1,
        name="finish",
        pinned=(True, False),
    )
    return (loss.reshape(()), vertex_grad, coeff_grad.reshape(shapes))


def solution(mesh):
    placed = (
        P("view"),
        P("view", None, "vertex"),
        P(None, "vertex"),
        P(None, "vertex"),
        P(("vertex", "view"), None, None),
        P(("vertex", "view"), None),
        P(("vertex", "view"), None),
        P(("vertex", "view"), None, None),
        P(("vertex", "view"), None),
        P(("vertex", "view"), None, None),
    )
    return jax.shard_map(
        per_device,
        mesh=mesh,
        in_specs=placed,
        out_specs=(P(), P(None, "vertex"), P("view")),
        check_vma=False,
    )
```

```python
import jax
import jax.numpy as jnp
from jax import lax
from jax.experimental import pallas as pl
from jax.experimental.pallas import tpu as pltpu
from jax.sharding import PartitionSpec as P

LANES = 128
SMOOTH = 0.1
VIEWS = 8
HOLDERS = 64
UNROLL_GATHER = 32
UNROLL_SCATTER = 16
OFFSETS = (-3, -2, -1, 0, 1, 2, 3, 32)
WIN = len(OFFSETS)
CAP = 4
COVER = 8
TILES = 32
BLOCKS = 16
PACKED = 40
SHARD = 24 + 3 * BLOCKS

F32 = jnp.float32
BF16 = jnp.bfloat16
VMEM = pl.BlockSpec(memory_space=pltpu.VMEM)
SMEM = pl.BlockSpec(memory_space=pltpu.SMEM)


def pick_lanes(source, lane):
    return jnp.take_along_axis(source, lane, axis=1, mode="promise_in_bounds")


def offset_kernel(
    u_ref, coeff_ref, basis_ref, rest_ref, corner_ref, fetch_ref, out_ref, shard_ref
):
    requests = jnp.maximum(fetch_ref[...], 0).astype(F32)
    holder = lax.broadcasted_iota(jnp.int32, requests.shape, 1)
    for v in range(VIEWS):
        mine = holder == ((u_ref[0] + OFFSETS[v]) & (HOLDERS - 1))
        wanted = jnp.sum(jnp.where(mine, requests, 0.0), axis=1, keepdims=True)
        out_ref[v, 24:28, :] = jnp.broadcast_to(wanted, (CAP, LANES))
        out_ref[v, 28:32, :] = jnp.zeros((CAP, LANES), F32)
    coeffs = jnp.broadcast_to(coeff_ref[...].astype(F32), (16, coeff_ref.shape[1])).astype(BF16)
    for d in range(3):
        row = jnp.dot(coeffs, basis_ref[d], preferred_element_type=F32)[0:1]
        for s in range(8):
            cols = slice(s * LANES, (s + 1) * LANES)
            for v in range(VIEWS):
                out_ref[v, 8 * d + s : 8 * d + s + 1, :] = row[:, cols]
            shard_ref[8 * d + s : 8 * d + s + 1, :] = rest_ref[d : d + 1, cols]
    for c in range(3):
        for b in range(BLOCKS):
            shard_ref[24 + c * BLOCKS + b : 25 + c * BLOCKS + b, :] = corner_ref[
                c : c + 1, b * LANES : (b + 1) * LANES
            ].astype(F32)


def pack_kernel(shard_ref, parts_ref, out_ref):
    wanted = jnp.concatenate([parts_ref[v, 24:28, :BLOCKS] for v in range(VIEWS)], axis=0)
    ids = lax.broadcasted_iota(jnp.int32, wanted.shape, 1)
    pick = jnp.where(wanted.astype(jnp.int32) == ids, 1.0, 0.0)
    for v in range(VIEWS):
        out_ref[v, 0:24, :] = shard_ref[0:24, :]
        out_ref[v, 36:40, :] = jnp.zeros((CAP, LANES), F32)
    for c in range(3):
        rows = jnp.dot(
            pick,
            shard_ref[24 + c * BLOCKS : 24 + (c + 1) * BLOCKS, :],
            precision=lax.Precision.HIGHEST,
            preferred_element_type=F32,
        )
        for v in range(VIEWS):
            out_ref[v, 24 + c * CAP : 24 + (c + 1) * CAP, :] = rows[v * CAP : (v + 1) * CAP]


def finish_kernel(pixels_ref, total_ref, grad_ref, coeff_ref, loss_ref, out_ref):
    shapes = coeff_ref.shape[1]
    coeff_ref[...] = total_ref[:, :shapes]
    loss_ref[...] = jnp.sum(total_ref[:, shapes:], axis=1, keepdims=True) * pixels_ref[0]
    out_ref[...] = grad_ref[...]


def lane_onehot(lane_row, ids):
    row = jnp.broadcast_to(lane_row.astype(F32), (16, LANES)).astype(BF16)
    one = jnp.ones((16, LANES), BF16)
    zero = jnp.zeros((16, LANES), BF16)
    return jnp.concatenate([jnp.where(i == row, one, zero) for i in ids], axis=0)


def dot_nt(a, b):
    return lax.dot_general(a, b, (((1,), (1,)), ((), ())), preferred_element_type=F32)


def entry_of(cover, u):
    relative = ((cover >> 2) - u + 3) & (HOLDERS - 1)
    return jnp.minimum(relative, WIN - 1) * CAP + (cover & (CAP - 1))


def tile_kernel(
    u_ref,
    cover_rows_ref,
    cover_line_ref,
    table_ref,
    slot_ref,
    weight_ref,
    camera_ref,
    target_ref,
    out_ref,
    energy_ref,
    entry_ref,
    entry_rows,
    sems,
    slot_rows,
    corner_id,
    entry_table,
    last_table,
    tile_last,
    corner_pix,
    last_pix,
    grad_pix,
    tile_grad,
    entry_grad,
):
    u = u_ref[0]
    entry_rows[...] = entry_of(cover_rows_ref[...], u) * 8
    entry_copy = pltpu.make_async_copy(entry_rows, entry_ref, sems.at[0])
    entry_copy.start()
    sub8 = lax.broadcasted_iota(jnp.int32, (8, LANES), 0)
    sub16 = lax.broadcasted_iota(jnp.int32, (16, LANES), 0)
    ids16 = [(sub16 + 16 * i).astype(F32).astype(BF16) for i in range(8)]
    for half in range(2):
        slot_rows[half * TILES : (half + 1) * TILES, :] = slot_ref[
            :, half * LANES : (half + 1) * LANES
        ]
    for j in range(WIN):
        corner_id[j * 16 : j * 16 + 16, :] = table_ref[j, 24:40, :].astype(jnp.int32)
    for j in range(WIN):
        ids = [corner_id[pl.ds(j * 16 + 8 * i, 8), :] for i in range(2)]
        lane = [i & (LANES - 1) for i in ids]
        sub = [i >> 7 for i in ids]
        for d in range(3):
            found = [jnp.zeros((8, LANES), F32)] * 2
            for s in range(8):
                source = jnp.broadcast_to(
                    table_ref[j, 8 * d + s : 8 * d + s + 1, :], (8, LANES)
                )
                for i in range(2):
                    found[i] = jnp.where(sub[i] == s, pick_lanes(source, lane[i]), found[i])
            for c in range(3):
                rows = found[c // 2][(c % 2) * CAP : (c % 2) * CAP + CAP]
                if 3 * c + d < 8:
                    entry_table[pl.ds(j * 32 + 3 * c + d, CAP, stride=8), :] = rows
                else:
                    last_table[pl.ds(j * 32, CAP, stride=8), :] = rows

    entry_copy.wait()

    def gather_tile(t, carry):
        entries = [entry_ref[n, t] for n in range(COVER)]
        base = pl.multiple_of(t * 8, 8)
        for n in range(COVER):
            tile_last[pl.ds(base + n, 1), :] = last_table[pl.ds(entries[n], 1), :]
        last = tile_last[pl.ds(base, 8), :]
        for half in range(2):
            q = slot_rows[pl.ds(half * TILES + t, 1), :]
            q = jnp.broadcast_to(q, (8, LANES))
            lane = q & (LANES - 1)
            which = q >> 7
            first = jnp.zeros((8, LANES), F32)
            for n in range(COVER):
                at = pl.multiple_of(entries[n], 8)
                picked = pick_lanes(entry_table[pl.ds(at, 8), :], lane)
                first = jnp.where(which == n, picked, first)
            second = jnp.where(which == sub8, pick_lanes(last, lane), 0.0)
            row = half * TILES + t
            corner_pix[pl.ds(pl.multiple_of(row * 8, 8), 8), :] = first
            last_pix[pl.ds(row, 1), :] = jnp.sum(second, axis=0, keepdims=True)
        return carry

    lax.fori_loop(0, TILES, gather_tile, 0, unroll=UNROLL_GATHER)

    camera = camera_ref[...].T
    energy = jnp.zeros((TILES, LANES), F32)
    for half in range(2):
        cols = slice(half * LANES, (half + 1) * LANES)
        weights = [weight_ref[c, :, cols] for c in range(3)]

        def rows_of(cd):
            return pl.ds(cd * 2 * TILES + half * TILES, TILES)

        def corner(cd):
            if cd == 8:
                return last_pix[half * TILES : (half + 1) * TILES, :]
            return corner_pix[pl.ds(half * TILES * 8 + cd, TILES, stride=8), :]

        surface = []
        for d in range(3):
            value = weights[0] * corner(d) + weights[1] * corner(3 + d)
            surface.append(value + weights[2] * corner(6 + d))
        grad_surface = [jnp.zeros((TILES, LANES), F32)] * 3
        for r in range(3):
            matrix = [camera[:, 3 * r + d : 3 * r + d + 1] for d in range(3)]
            linear = matrix[0] * surface[0]
            linear = linear + matrix[1] * surface[1]
            linear = linear + matrix[2] * surface[2]
            shaded = jnp.tanh(linear + camera[:, 9 + r : 10 + r])
            differ = shaded - target_ref[r, :, cols]
            square = differ * differ + SMOOTH * SMOOTH
            inverse = lax.rsqrt(square)
            energy = energy + square * inverse
            grad_linear = differ * inverse * (1.0 - shaded * shaded)
            for d in range(3):
                grad_surface[d] = grad_surface[d] + matrix[d] * grad_linear
        for c in range(3):
            for d in range(3):
                grad = weights[c] * grad_surface[d]
                high = grad.astype(BF16).astype(F32)
                grad_pix[rows_of(3 * c + d), :] = high
                grad_pix[rows_of(9 + 3 * c + d), :] = grad - high
    energy_ref[...] = energy[0:8] + energy[8:16] + energy[16:24] + energy[24:32]

    def scatter_tile(t, carry):
        spread_rows = [[] for _ in range(18)]
        onehot = []
        for half in range(2):
            q = slot_rows[pl.ds(half * TILES + t, 1), :]
            mine = jnp.broadcast_to(q >> 7, (8, LANES)) == sub8
            onehot.append(lane_onehot(q & (LANES - 1), ids16))
            for cd in range(18):
                grad = grad_pix[pl.ds(cd * 2 * TILES + half * TILES + t, 1), :]
                grad = jnp.broadcast_to(grad, (8, LANES))
                spread_rows[cd].append(jnp.where(mine, grad, 0.0))
        rows = jnp.concatenate([jnp.concatenate(r, axis=1) for r in spread_rows], axis=0)
        summed = dot_nt(rows.astype(BF16), jnp.concatenate(onehot, axis=1))
        summed = summed[:72] + summed[72:]
        for cd in range(9):
            at = pl.multiple_of(cd * COVER * TILES + t * COVER, COVER)
            tile_grad[pl.ds(at, COVER), :] = summed[8 * cd : 8 * cd + 8]
        return carry

    lax.fori_loop(0, TILES, scatter_tile, 0, unroll=UNROLL_SCATTER)

    entry_line = entry_of(cover_line_ref[...], u)
    entry_ids = lax.broadcasted_iota(jnp.int32, (WIN * CAP, TILES * COVER), 0)
    pick = jnp.where(entry_ids == entry_line, 1.0, 0.0).astype(BF16)
    for cd in range(9):
        values = tile_grad[pl.ds(cd * COVER * TILES, COVER * TILES), :]
        high = values.astype(BF16)
        low = (values - high.astype(F32)).astype(BF16)
        both = jnp.dot(
            pick, jnp.concatenate([high, low], axis=1), preferred_element_type=F32
        )
        both = both[:, :LANES] + both[:, LANES:]
        high = both.astype(BF16).astype(F32)
        entry_grad[pl.ds(cd * WIN * CAP, WIN * CAP), :] = high
        entry_grad[pl.ds((9 + cd) * WIN * CAP, WIN * CAP), :] = both - high

    for j in range(WIN):
        rows = [[] for _ in range(6)]
        onehot = []
        for c in range(3):
            for s in range(CAP):
                ids = corner_id[pl.ds(j * 16 + c * CAP + s, 1), :]
                mine = jnp.broadcast_to(ids >> 7, (8, LANES)) == sub8
                onehot.append(lane_onehot(ids & (LANES - 1), ids16))
                for d in range(6):
                    at = (9 * (d // 3) + 3 * c + d % 3) * WIN * CAP + j * CAP + s
                    grad = jnp.broadcast_to(entry_grad[pl.ds(at, 1), :], (8, LANES))
                    rows[d].append(jnp.where(mine, grad, 0.0))
        stacked = jnp.concatenate([jnp.concatenate(r, axis=1) for r in rows], axis=0)
        summed = dot_nt(stacked.astype(BF16), jnp.concatenate(onehot, axis=1))
        out_ref[j] = summed[:24] + summed[24:]


def call(kernel, out_shapes, args, scalars=0, scratch=(), name=None, pinned=(True, True)):
    if pinned[0]:
        args = args[:scalars] + tuple(
            pltpu.with_memory_space_constraint(a, pltpu.VMEM) for a in args[scalars:]
        )
    kind = pltpu.VMEM if pinned[1] else jax.ShapeDtypeStruct
    return pl.pallas_call(
        kernel,
        out_shape=[kind(s, F32) for s in out_shapes],
        in_specs=[SMEM] * scalars + [VMEM] * (len(args) - scalars),
        out_specs=[VMEM] * len(out_shapes),
        scratch_shapes=list(scratch),
        name=name,
        compiler_params=pltpu.CompilerParams(),
    )(*args)


def exchange(array, axis):
    return lax.all_to_all(array, axis, 0, 0, tiled=True)


def tile_call(u, tile_cover, cover_line, table, pix_slot, barycentric, camera, target):
    return call(
        tile_kernel,
        [(WIN, 24, LANES), (8, LANES)],
        (
            u.reshape(1),
            jnp.transpose(tile_cover),
            cover_line,
            table,
            pix_slot,
            barycentric,
            camera,
            target,
        ),
        scalars=1,
        scratch=(
            pltpu.SMEM((COVER, TILES), jnp.int32),
            pltpu.VMEM((COVER, TILES), jnp.int32),
            pltpu.SemaphoreType.DMA((1,)),
            pltpu.VMEM((2 * TILES, LANES), jnp.int32),
            pltpu.VMEM((16 * WIN, LANES), jnp.int32),
            pltpu.VMEM((8 * WIN * CAP, LANES), F32),
            pltpu.VMEM((8 * WIN * CAP, LANES), F32),
            pltpu.VMEM((8 * TILES, LANES), F32),
            pltpu.VMEM((8 * 2 * TILES, LANES), F32),
            pltpu.VMEM((2 * TILES, LANES), F32),
            pltpu.VMEM((18 * 2 * TILES, LANES), F32),
            pltpu.VMEM((9 * TILES * COVER, LANES), F32),
            pltpu.VMEM((18 * WIN * CAP, LANES), F32),
        ),
        name="tiles",
    )


def to_all(array, axis):
    size = lax.axis_size(axis)
    return exchange(jnp.broadcast_to(array[None], (size, *array.shape)), axis)


def along_window(array, sign):
    holders = lax.axis_size("vertex")
    pairs = [
        (h * VIEWS + j, (h + sign * OFFSETS[j]) % holders * VIEWS + j)
        for h in range(holders)
        for j in range(VIEWS)
    ]
    return lax.ppermute(array, ("vertex", "view"), pairs)


def per_device(
    coeffs,
    shape_basis,
    rest_pose,
    triangles,
    fetch_list,
    tile_cover,
    pix_slot,
    barycentric,
    camera,
    target,
):
    u = lax.axis_index("vertex").astype(jnp.int32)
    pixels = (
        tile_cover.shape[0] * pix_slot.shape[1] * lax.axis_size("vertex") * lax.axis_size("view")
    )
    shapes = coeffs.shape[0]
    basis = jnp.transpose(shape_basis, (1, 0, 2))
    partial, shard = call(
        offset_kernel,
        [(VIEWS, 32, LANES), (SHARD, LANES)],
        (
            u.reshape(1),
            coeffs.reshape(1, shapes),
            basis,
            rest_pose,
            triangles,
            jnp.transpose(fetch_list[0]),
        ),
        scalars=1,
        name="offsets",
        pinned=(False, True),
    )
    parts = exchange(partial, "view")
    offsets = parts[:, :24].sum(axis=0)
    shard = shard + jnp.pad(offsets, ((0, SHARD - 24), (0, 0)))
    shard = along_window(shard, -1)
    cover_line = tile_cover.reshape(1, TILES * COVER)
    lens = jnp.pad(jnp.transpose(camera), ((0, 4), (0, 0)))
    shard, cover_line, lens, u = lax.optimization_barrier((shard, cover_line, lens, u))
    packed = call(pack_kernel, [(VIEWS, PACKED, LANES)], (shard, parts), name="pack")[0]
    table = exchange(packed, "view")
    grads, energy = tile_call(
        u,
        tile_cover,
        cover_line,
        table,
        pix_slot,
        jnp.transpose(barycentric, (1, 0, 2)),
        lens,
        jnp.transpose(target, (1, 0, 2)),
    )
    returned = along_window(exchange(grads, "view").sum(axis=0), 1)
    total = to_all(jnp.concatenate([returned, energy], axis=0), "view").sum(axis=0)
    vertex_grad = total[:24].reshape(3, VIEWS * LANES)
    coeff_part = jnp.sum(basis.astype(F32) * vertex_grad[:, None, :], axis=(0, 2))
    energy_part = total[24:].sum(axis=0)
    energy_part = energy_part[:shapes] + energy_part[shapes:]
    rows = jnp.concatenate([coeff_part, energy_part]).reshape(1, 2 * shapes)
    total = to_all(rows, "vertex").sum(axis=0)
    coeff_grad, loss, vertex_grad = call(
        finish_kernel,
        [(1, shapes), (1, 1), vertex_grad.shape],
        (jnp.full((1,), 1.0 / pixels, F32), total, vertex_grad),
        scalars=1,
        name="finish",
        pinned=(True, False),
    )
    return (loss.reshape(()), vertex_grad, coeff_grad.reshape(shapes))


def solution(mesh):
    placed = (
        P("view"),
        P("view", None, "vertex"),
        P(None, "vertex"),
        P(None, "vertex"),
        P(("vertex", "view"), None, None),
        P(("vertex", "view"), None),
        P(("vertex", "view"), None),
        P(("vertex", "view"), None, None),
        P(("vertex", "view"), None),
        P(("vertex", "view"), None, None),
    )
    return jax.shard_map(
        per_device,
        mesh=mesh,
        in_specs=placed,
        out_specs=(P(), P(None, "vertex"), P("view")),
        check_vma=False,
    )
```

```python
import jax
import jax.numpy as jnp
from jax import lax
from jax.experimental import pallas as pl
from jax.experimental.pallas import tpu as pltpu
from jax.sharding import PartitionSpec as P

LANES = 128
SMOOTH = 0.1
VIEWS = 8
HOLDERS = 64
UNROLL_GATHER = 32
UNROLL_SCATTER = 16
OFFSETS = (-3, 3, -2, 2, -1, 1, 0, 32)
WIN = len(OFFSETS)
CAP = 4
COVER = 8
TILES = 32
BLOCKS = 16
PACKED = 40
SHARD = 24 + 3 * BLOCKS

F32 = jnp.float32
BF16 = jnp.bfloat16
VMEM = pl.BlockSpec(memory_space=pltpu.VMEM)
SMEM = pl.BlockSpec(memory_space=pltpu.SMEM)


def pick_lanes(source, lane):
    return jnp.take_along_axis(source, lane, axis=1, mode="promise_in_bounds")


def offset_kernel(
    u_ref, coeff_ref, basis_ref, rest_ref, corner_ref, fetch_ref, out_ref, shard_ref
):
    requests = jnp.maximum(fetch_ref[...], 0).astype(F32)
    holder = lax.broadcasted_iota(jnp.int32, requests.shape, 1)
    for v in range(VIEWS):
        mine = holder == ((u_ref[0] + OFFSETS[v]) & (HOLDERS - 1))
        wanted = jnp.sum(jnp.where(mine, requests, 0.0), axis=1, keepdims=True)
        out_ref[v, 24:28, :] = jnp.broadcast_to(wanted, (CAP, LANES))
        out_ref[v, 28:32, :] = jnp.zeros((CAP, LANES), F32)
    coeffs = jnp.broadcast_to(coeff_ref[...].astype(F32), (16, coeff_ref.shape[1])).astype(BF16)
    for d in range(3):
        row = jnp.dot(coeffs, basis_ref[d], preferred_element_type=F32)[0:1]
        for s in range(8):
            cols = slice(s * LANES, (s + 1) * LANES)
            for v in range(VIEWS):
                out_ref[v, 8 * d + s : 8 * d + s + 1, :] = row[:, cols]
            shard_ref[8 * d + s : 8 * d + s + 1, :] = rest_ref[d : d + 1, cols]
    for c in range(3):
        for b in range(BLOCKS):
            shard_ref[24 + c * BLOCKS + b : 25 + c * BLOCKS + b, :] = corner_ref[
                c : c + 1, b * LANES : (b + 1) * LANES
            ].astype(F32)


def pack_kernel(shard_ref, parts_ref, out_ref):
    wanted = jnp.concatenate([parts_ref[v, 24:28, :BLOCKS] for v in range(VIEWS)], axis=0)
    ids = lax.broadcasted_iota(jnp.int32, wanted.shape, 1)
    pick = jnp.where(wanted.astype(jnp.int32) == ids, 1.0, 0.0)
    for v in range(VIEWS):
        out_ref[v, 0:24, :] = shard_ref[0:24, :]
        out_ref[v, 36:40, :] = jnp.zeros((CAP, LANES), F32)
    for c in range(3):
        rows = jnp.dot(
            pick,
            shard_ref[24 + c * BLOCKS : 24 + (c + 1) * BLOCKS, :],
            precision=lax.Precision.HIGHEST,
            preferred_element_type=F32,
        )
        for v in range(VIEWS):
            out_ref[v, 24 + c * CAP : 24 + (c + 1) * CAP, :] = rows[v * CAP : (v + 1) * CAP]


def finish_kernel(pixels_ref, total_ref, grad_ref, coeff_ref, loss_ref, out_ref):
    shapes = coeff_ref.shape[1]
    coeff_ref[...] = total_ref[:, :shapes]
    loss_ref[...] = jnp.sum(total_ref[:, shapes:], axis=1, keepdims=True) * pixels_ref[0]
    out_ref[...] = grad_ref[...]


def lane_onehot(lane_row, ids):
    row = jnp.broadcast_to(lane_row.astype(F32), (16, LANES)).astype(BF16)
    one = jnp.ones((16, LANES), BF16)
    zero = jnp.zeros((16, LANES), BF16)
    return jnp.concatenate([jnp.where(i == row, one, zero) for i in ids], axis=0)


def dot_nt(a, b):
    return lax.dot_general(a, b, (((1,), (1,)), ((), ())), preferred_element_type=F32)


def entry_of(cover, u):
    step = jnp.minimum(((cover >> 2) - u + 3) & (HOLDERS - 1), 7) - 3
    slot = jnp.where(step < 0, 2 * step + 6, 7 - 2 * step)
    slot = jnp.where(step == 0, 6, jnp.where(step == 4, 7, slot))
    return slot * CAP + (cover & (CAP - 1))


def tile_kernel(
    u_ref,
    cover_rows_ref,
    cover_line_ref,
    table_ref,
    slot_ref,
    weight_ref,
    camera_ref,
    target_ref,
    out_ref,
    energy_ref,
    entry_ref,
    entry_rows,
    sems,
    slot_rows,
    corner_id,
    entry_table,
    last_table,
    tile_last,
    corner_pix,
    last_pix,
    grad_pix,
    tile_grad,
    entry_grad,
):
    u = u_ref[0]
    entry_rows[...] = entry_of(cover_rows_ref[...], u) * 8
    entry_copy = pltpu.make_async_copy(entry_rows, entry_ref, sems.at[0])
    entry_copy.start()
    sub8 = lax.broadcasted_iota(jnp.int32, (8, LANES), 0)
    sub16 = lax.broadcasted_iota(jnp.int32, (16, LANES), 0)
    ids16 = [(sub16 + 16 * i).astype(F32).astype(BF16) for i in range(8)]
    for half in range(2):
        slot_rows[half * TILES : (half + 1) * TILES, :] = slot_ref[
            :, half * LANES : (half + 1) * LANES
        ]
    for j in range(WIN):
        corner_id[j * 16 : j * 16 + 16, :] = table_ref[j, 24:40, :].astype(jnp.int32)
    for j in range(WIN):
        ids = [corner_id[pl.ds(j * 16 + 8 * i, 8), :] for i in range(2)]
        lane = [i & (LANES - 1) for i in ids]
        sub = [i >> 7 for i in ids]
        for d in range(3):
            found = [jnp.zeros((8, LANES), F32)] * 2
            for s in range(8):
                source = jnp.broadcast_to(
                    table_ref[j, 8 * d + s : 8 * d + s + 1, :], (8, LANES)
                )
                for i in range(2):
                    found[i] = jnp.where(sub[i] == s, pick_lanes(source, lane[i]), found[i])
            for c in range(3):
                rows = found[c // 2][(c % 2) * CAP : (c % 2) * CAP + CAP]
                if 3 * c + d < 8:
                    entry_table[pl.ds(j * 32 + 3 * c + d, CAP, stride=8), :] = rows
                else:
                    last_table[pl.ds(j * 32, CAP, stride=8), :] = rows

    entry_copy.wait()

    def gather_tile(t, carry):
        entries = [entry_ref[n, t] for n in range(COVER)]
        base = pl.multiple_of(t * 8, 8)
        for n in range(COVER):
            tile_last[pl.ds(base + n, 1), :] = last_table[pl.ds(entries[n], 1), :]
        last = tile_last[pl.ds(base, 8), :]
        for half in range(2):
            q = slot_rows[pl.ds(half * TILES + t, 1), :]
            q = jnp.broadcast_to(q, (8, LANES))
            lane = q & (LANES - 1)
            which = q >> 7
            first = jnp.zeros((8, LANES), F32)
            for n in range(COVER):
                at = pl.multiple_of(entries[n], 8)
                picked = pick_lanes(entry_table[pl.ds(at, 8), :], lane)
                first = jnp.where(which == n, picked, first)
            second = jnp.where(which == sub8, pick_lanes(last, lane), 0.0)
            row = half * TILES + t
            corner_pix[pl.ds(pl.multiple_of(row * 8, 8), 8), :] = first
            last_pix[pl.ds(row, 1), :] = jnp.sum(second, axis=0, keepdims=True)
        return carry

    lax.fori_loop(0, TILES, gather_tile, 0, unroll=UNROLL_GATHER)

    camera = camera_ref[...].T
    energy = jnp.zeros((TILES, LANES), F32)
    for half in range(2):
        cols = slice(half * LANES, (half + 1) * LANES)
        weights = [weight_ref[c, :, cols] for c in range(3)]

        def rows_of(cd):
            return pl.ds(cd * 2 * TILES + half * TILES, TILES)

        def corner(cd):
            if cd == 8:
                return last_pix[half * TILES : (half + 1) * TILES, :]
            return corner_pix[pl.ds(half * TILES * 8 + cd, TILES, stride=8), :]

        surface = []
        for d in range(3):
            value = weights[0] * corner(d) + weights[1] * corner(3 + d)
            surface.append(value + weights[2] * corner(6 + d))
        grad_surface = [jnp.zeros((TILES, LANES), F32)] * 3
        for r in range(3):
            matrix = [camera[:, 3 * r + d : 3 * r + d + 1] for d in range(3)]
            linear = matrix[0] * surface[0]
            linear = linear + matrix[1] * surface[1]
            linear = linear + matrix[2] * surface[2]
            shaded = jnp.tanh(linear + camera[:, 9 + r : 10 + r])
            differ = shaded - target_ref[r, :, cols]
            square = differ * differ + SMOOTH * SMOOTH
            inverse = lax.rsqrt(square)
            energy = energy + square * inverse
            grad_linear = differ * inverse * (1.0 - shaded * shaded)
            for d in range(3):
                grad_surface[d] = grad_surface[d] + matrix[d] * grad_linear
        for c in range(3):
            for d in range(3):
                grad = weights[c] * grad_surface[d]
                high = grad.astype(BF16).astype(F32)
                grad_pix[rows_of(3 * c + d), :] = high
                grad_pix[rows_of(9 + 3 * c + d), :] = grad - high
    energy_ref[...] = energy[0:8] + energy[8:16] + energy[16:24] + energy[24:32]

    def scatter_tile(t, carry):
        spread_rows = [[] for _ in range(18)]
        onehot = []
        for half in range(2):
            q = slot_rows[pl.ds(half * TILES + t, 1), :]
            mine = jnp.broadcast_to(q >> 7, (8, LANES)) == sub8
            onehot.append(lane_onehot(q & (LANES - 1), ids16))
            for cd in range(18):
                grad = grad_pix[pl.ds(cd * 2 * TILES + half * TILES + t, 1), :]
                grad = jnp.broadcast_to(grad, (8, LANES))
                spread_rows[cd].append(jnp.where(mine, grad, 0.0))
        rows = jnp.concatenate([jnp.concatenate(r, axis=1) for r in spread_rows], axis=0)
        summed = dot_nt(rows.astype(BF16), jnp.concatenate(onehot, axis=1))
        summed = summed[:72] + summed[72:]
        for cd in range(9):
            at = pl.multiple_of(cd * COVER * TILES + t * COVER, COVER)
            tile_grad[pl.ds(at, COVER), :] = summed[8 * cd : 8 * cd + 8]
        return carry

    lax.fori_loop(0, TILES, scatter_tile, 0, unroll=UNROLL_SCATTER)

    entry_line = entry_of(cover_line_ref[...], u)
    entry_ids = lax.broadcasted_iota(jnp.int32, (WIN * CAP, TILES * COVER), 0)
    pick = jnp.where(entry_ids == entry_line, 1.0, 0.0).astype(BF16)
    for cd in range(9):
        values = tile_grad[pl.ds(cd * COVER * TILES, COVER * TILES), :]
        high = values.astype(BF16)
        low = (values - high.astype(F32)).astype(BF16)
        both = jnp.dot(
            pick, jnp.concatenate([high, low], axis=1), preferred_element_type=F32
        )
        both = both[:, :LANES] + both[:, LANES:]
        high = both.astype(BF16).astype(F32)
        entry_grad[pl.ds(cd * WIN * CAP, WIN * CAP), :] = high
        entry_grad[pl.ds((9 + cd) * WIN * CAP, WIN * CAP), :] = both - high

    for j in range(WIN):
        rows = [[] for _ in range(6)]
        onehot = []
        for c in range(3):
            for s in range(CAP):
                ids = corner_id[pl.ds(j * 16 + c * CAP + s, 1), :]
                mine = jnp.broadcast_to(ids >> 7, (8, LANES)) == sub8
                onehot.append(lane_onehot(ids & (LANES - 1), ids16))
                for d in range(6):
                    at = (9 * (d // 3) + 3 * c + d % 3) * WIN * CAP + j * CAP + s
                    grad = jnp.broadcast_to(entry_grad[pl.ds(at, 1), :], (8, LANES))
                    rows[d].append(jnp.where(mine, grad, 0.0))
        stacked = jnp.concatenate([jnp.concatenate(r, axis=1) for r in rows], axis=0)
        summed = dot_nt(stacked.astype(BF16), jnp.concatenate(onehot, axis=1))
        out_ref[j] = summed[:24] + summed[24:]


def call(kernel, out_shapes, args, scalars=0, scratch=(), name=None, pinned=(True, True)):
    if pinned[0]:
        args = args[:scalars] + tuple(
            pltpu.with_memory_space_constraint(a, pltpu.VMEM) for a in args[scalars:]
        )
    kind = pltpu.VMEM if pinned[1] else jax.ShapeDtypeStruct
    return pl.pallas_call(
        kernel,
        out_shape=[kind(s, F32) for s in out_shapes],
        in_specs=[SMEM] * scalars + [VMEM] * (len(args) - scalars),
        out_specs=[VMEM] * len(out_shapes),
        scratch_shapes=list(scratch),
        name=name,
        compiler_params=pltpu.CompilerParams(),
    )(*args)


def exchange(array, axis):
    return lax.all_to_all(array, axis, 0, 0, tiled=True)


def tile_call(u, tile_cover, cover_line, table, pix_slot, barycentric, camera, target):
    return call(
        tile_kernel,
        [(WIN, 24, LANES), (8, LANES)],
        (
            u.reshape(1),
            jnp.transpose(tile_cover),
            cover_line,
            table,
            pix_slot,
            barycentric,
            camera,
            target,
        ),
        scalars=1,
        scratch=(
            pltpu.SMEM((COVER, TILES), jnp.int32),
            pltpu.VMEM((COVER, TILES), jnp.int32),
            pltpu.SemaphoreType.DMA((1,)),
            pltpu.VMEM((2 * TILES, LANES), jnp.int32),
            pltpu.VMEM((16 * WIN, LANES), jnp.int32),
            pltpu.VMEM((8 * WIN * CAP, LANES), F32),
            pltpu.VMEM((8 * WIN * CAP, LANES), F32),
            pltpu.VMEM((8 * TILES, LANES), F32),
            pltpu.VMEM((8 * 2 * TILES, LANES), F32),
            pltpu.VMEM((2 * TILES, LANES), F32),
            pltpu.VMEM((18 * 2 * TILES, LANES), F32),
            pltpu.VMEM((9 * TILES * COVER, LANES), F32),
            pltpu.VMEM((18 * WIN * CAP, LANES), F32),
        ),
        name="tiles",
    )


def to_all(array, axis):
    size = lax.axis_size(axis)
    return exchange(jnp.broadcast_to(array[None], (size, *array.shape)), axis)


def along_window(array, sign):
    holders = lax.axis_size("vertex")
    pairs = [
        (h * VIEWS + j, (h + sign * OFFSETS[j]) % holders * VIEWS + j)
        for h in range(holders)
        for j in range(VIEWS)
    ]
    return lax.ppermute(array, ("vertex", "view"), pairs)


def per_device(
    coeffs,
    shape_basis,
    rest_pose,
    triangles,
    fetch_list,
    tile_cover,
    pix_slot,
    barycentric,
    camera,
    target,
):
    u = lax.axis_index("vertex").astype(jnp.int32)
    pixels = (
        tile_cover.shape[0] * pix_slot.shape[1] * lax.axis_size("vertex") * lax.axis_size("view")
    )
    shapes = coeffs.shape[0]
    basis = jnp.transpose(shape_basis, (1, 0, 2))
    partial, shard = call(
        offset_kernel,
        [(VIEWS, 32, LANES), (SHARD, LANES)],
        (
            u.reshape(1),
            coeffs.reshape(1, shapes),
            basis,
            rest_pose,
            triangles,
            jnp.transpose(fetch_list[0]),
        ),
        scalars=1,
        name="offsets",
        pinned=(False, True),
    )
    parts = exchange(partial, "view")
    offsets = parts[:, :24].sum(axis=0)
    shard = shard + jnp.pad(offsets, ((0, SHARD - 24), (0, 0)))
    shard = along_window(shard, -1)
    cover_line = tile_cover.reshape(1, TILES * COVER)
    lens = jnp.pad(jnp.transpose(camera), ((0, 4), (0, 0)))
    shard, cover_line, lens, u = lax.optimization_barrier((shard, cover_line, lens, u))
    packed = call(pack_kernel, [(VIEWS, PACKED, LANES)], (shard, parts), name="pack")[0]
    table = exchange(packed, "view")
    grads, energy = tile_call(
        u,
        tile_cover,
        cover_line,
        table,
        pix_slot,
        jnp.transpose(barycentric, (1, 0, 2)),
        lens,
        jnp.transpose(target, (1, 0, 2)),
    )
    returned = along_window(exchange(grads, "view").sum(axis=0), 1)
    total = to_all(jnp.concatenate([returned, energy], axis=0), "view").sum(axis=0)
    vertex_grad = total[:24].reshape(3, VIEWS * LANES)
    coeff_part = jnp.sum(basis.astype(F32) * vertex_grad[:, None, :], axis=(0, 2))
    energy_part = total[24:].sum(axis=0)
    energy_part = energy_part[:shapes] + energy_part[shapes:]
    rows = jnp.concatenate([coeff_part, energy_part]).reshape(1, 2 * shapes)
    total = to_all(rows, "vertex").sum(axis=0)
    coeff_grad, loss, vertex_grad = call(
        finish_kernel,
        [(1, shapes), (1, 1), vertex_grad.shape],
        (jnp.full((1,), 1.0 / pixels, F32), total, vertex_grad),
        scalars=1,
        name="finish",
        pinned=(True, False),
    )
    return (loss.reshape(()), vertex_grad, coeff_grad.reshape(shapes))


def solution(mesh):
    placed = (
        P("view"),
        P("view", None, "vertex"),
        P(None, "vertex"),
        P(None, "vertex"),
        P(("vertex", "view"), None, None),
        P(("vertex", "view"), None),
        P(("vertex", "view"), None),
        P(("vertex", "view"), None, None),
        P(("vertex", "view"), None),
        P(("vertex", "view"), None, None),
    )
    return jax.shard_map(
        per_device,
        mesh=mesh,
        in_specs=placed,
        out_specs=(P(), P(None, "vertex"), P("view")),
        check_vma=False,
    )
```
